512 devices in a mesh: ka: 128 (over y, x_hi, z), ta: 4 (over x_lo, core).
Axes of the slice: x: 4 (x_hi: 2, x_lo: 2; x = x_hi * 2 + x_lo), y: 8, z: 8, core: 2. Of those that a mesh axis runs over, the one named last changes fastest.
Arguments:
- green_hist: bfloat16 [256, 2, 2, 2, 512, 512], P('ka', None, None, None, 'ta'), may hold values from -6 to 6
- sigma_hist: bfloat16 [2, 2, 2, 512, 512], P(None, None, None, 'ta'), may hold values from -6 to 6
- prev_row: float32 [256, 2, 2, 2, 512], P('ka', None, None, None, 'ta'), may hold values from -8 to 8
- propagator: float32 [256, 2, 2, 2], P('ka'), may hold values from -3 to 3
- impurity_column: float32 [2, 2, 2, 512], P(None, None, None, 'ta'), may hold values from -3 to 3
- sigma_start: float32 [2, 2, 2, 512], P(None, None, None, 'ta'), may hold values from -6 to 6
Outputs:
- green_row: float32 [256, 2, 2, 2, 512], P('ka', None, None, None, 'ta')
- self_energy: float32 [2, 2, 2, 512], P(None, None, None, 'ta')
The draws below stay inside these ranges and needn't reach their ends.
All inputs are finite; a program needn't handle non-finite values.
Results may differ from the reference program's by a relative error of at most 0.0031.
Values sent between devices are 32-bit elements; how exact they have to be, the bound alone decides.
No kernel may reach another device: no remote copies, remote signals or barrier semaphores. Data moves between devices by JAX's collectives and lax.ppermute only.
A program may use at most 64 MiB of HBM per device.

```python
import jax
import jax.numpy as jnp
from jax import lax

H = 512
ITERS = 2
KPTS = 256


def draw_prev_row(key, part):
    common_key = jax.random.fold_in(key, 11)
    noise_key = jax.random.fold_in(key, 12)
    common = jax.random.normal(common_key, (1, 2, 2, 2, H), jnp.float32)
    noise = 0.5 * jax.random.normal(noise_key, (KPTS, 2, 2, 2, H), jnp.float32)
    return jnp.clip(common + noise, -8.0, 8.0)


def draw_propagator(key, part):
    noise_key = jax.random.fold_in(key, 21)
    noise = 0.3 * jax.random.normal(noise_key, (KPTS, 2, 2, 2), jnp.float32)
    identity = (jnp.arange(2)[:, None] == jnp.arange(2)[None, :]).astype(jnp.float32)
    base = jnp.stack([identity, jnp.zeros((2, 2), jnp.float32)], axis=0)
    return jnp.clip(base[None] + noise, -3.0, 3.0)


def levels(own_key, extent, cuts, smallest, high):
    gain, own = 1.0, jax.random.fold_in(own_key, 6)
    for position, shards_of in cuts:
        heights = jnp.exp(jax.random.uniform(jax.random.fold_in(own, position), (shards_of,), jnp.float32, smallest / len(cuts), high / len(cuts)))
        gain = gain * jnp.repeat(heights, extent[position] // shards_of).reshape([-1 if axis == position else 1 for axis in range(len(extent))])
    return gain


def scatter_about(key, shape, width, limit, split=(), dtype=jnp.bfloat16):
    result = width * jax.random.normal(key, shape, jnp.float32)
    if split:
        result = result * levels(key, shape, split, -0.22, 0.18)
    return jnp.clip(result, -limit, limit).astype(dtype)


def setup_inputs(seed: int = 0) -> dict:
    splits = jax.random.split(jax.random.key(seed), 7)
    green_hist = scatter_about(splits[0], (KPTS, 2, 2, 2, H, H), 1.0, 6.0, ((0, 128), (4, 4)))
    sigma_hist = scatter_about(splits[1], (2, 2, 2, H, H), 1.0, 6.0, ((3, 4),))
    prev_row = draw_prev_row(jax.random.fold_in(splits[6], 71), 0)
    propagator = draw_propagator(jax.random.fold_in(splits[6], 71), 0)
    impurity_column = scatter_about(splits[4], (2, 2, 2, H), 0.5, 3.0, ((3, 4),), jnp.float32)
    sigma_start = scatter_about(splits[5], (2, 2, 2, H), 1.0, 6.0, ((3, 4),), jnp.float32)
    return dict(green_hist=green_hist, sigma_hist=sigma_hist, prev_row=prev_row, propagator=propagator, impurity_column=impurity_column, sigma_start=sigma_start)


TIME_STEP = 0.02
COUPLING = 1.0


def sigma_block(self_energy):
    real_part = self_energy[0]
    imag_part = self_energy[1]
    upper = jnp.stack([real_part, -imag_part], axis=1)
    lower = jnp.stack([imag_part, real_part], axis=1)
    return jnp.stack([upper, lower], axis=0)


def row_block(green_row):
    real_part = green_row[:, 0]
    imag_part = green_row[:, 1]
    upper = jnp.stack([real_part, -imag_part], axis=2)
    lower = jnp.stack([imag_part, real_part], axis=2)
    return jnp.stack([upper, lower], axis=1)


def orbital_product(left, right):
    return jnp.sum(left[:, :, :, None, None] * right[:, None, :, :, :], axis=2)


def propagate(propagator, inner):
    prop_real = propagator[:, 0]
    prop_imag = propagator[:, 1]
    inner_real = inner[:, 0]
    inner_imag = inner[:, 1]
    real_part = orbital_product(prop_real, inner_real) - orbital_product(prop_imag, inner_imag)
    imag_part = orbital_product(prop_real, inner_imag) + orbital_product(prop_imag, inner_real)
    return jnp.stack([real_part, imag_part], axis=1)


def second_order(local_green, column):
    green_real = local_green[0]
    green_imag = local_green[1]
    square_real = green_real * green_real - green_imag * green_imag
    square_imag = 2.0 * green_real * green_imag
    real_part = square_real * column[0] - square_imag * column[1]
    imag_part = square_real * column[1] + square_imag * column[0]
    return COUPLING * COUPLING * jnp.stack([real_part, imag_part], axis=0)


def reference(green_hist, sigma_hist, prev_row, propagator, impurity_column, sigma_start):
    green_row = prev_row
    self_energy = sigma_start
    sigma_wide = sigma_hist.astype(jnp.float32)
    for iteration in range(ITERS):
        block = lax.optimization_barrier(sigma_block(self_energy).astype(jnp.bfloat16)).astype(jnp.float32)

        def one_point(history):
            return jnp.einsum('oarbs,rbcst->oact', block, history.astype(jnp.float32))

        term_one = lax.map(one_point, green_hist)
        rows_low = lax.optimization_barrier(row_block(green_row).astype(jnp.bfloat16)).astype(jnp.float32)
        term_two = jnp.einsum('koarbs,rbcst->koact', rows_low, sigma_wide)
        green_row = propagate(propagator, prev_row + TIME_STEP * (term_one + term_two))
        local_green = jnp.sum(green_row, axis=0) / KPTS
        self_energy = second_order(local_green, impurity_column)
    return green_row, self_energy
```

```python
import jax
import jax.numpy as jnp
from jax import lax
from jax.sharding import Mesh, PartitionSpec as P

ITERS = 2


TIME_STEP = 0.02
COUPLING = 1.0

CUT = (("yh", 4), ("yl", 2), ("xh", 2), ("z", 8), ("xl", 2), ("core", 2))
KA = ("yh", "yl", "xh", "z")
TA = ("xl", "core")
NEAR = ("yl", "xh")
FAR = ("yh", "z")


def sigma_block(self_energy):
    real_part = self_energy[0]
    imag_part = self_energy[1]
    upper = jnp.stack([real_part, -imag_part], axis=1)
    lower = jnp.stack([imag_part, real_part], axis=1)
    return jnp.stack([upper, lower], axis=0)


def row_block(green_row):
    real_part = green_row[:, 0]
    imag_part = green_row[:, 1]
    upper = jnp.stack([real_part, -imag_part], axis=2)
    lower = jnp.stack([imag_part, real_part], axis=2)
    return jnp.stack([upper, lower], axis=1)


def orbital_product(left, right):
    return jnp.sum(left[:, :, :, None, None] * right[:, None, :, :, :], axis=2)


def propagate(propagator, inner):
    prop_real = propagator[:, 0]
    prop_imag = propagator[:, 1]
    inner_real = inner[:, 0]
    inner_imag = inner[:, 1]
    real_part = orbital_product(prop_real, inner_real) - orbital_product(prop_imag, inner_imag)
    imag_part = orbital_product(prop_real, inner_imag) + orbital_product(prop_imag, inner_real)
    return jnp.stack([real_part, imag_part], axis=1)


def second_order(local_green, column):
    green_real = local_green[0]
    green_imag = local_green[1]
    square_real = green_real * green_real - green_imag * green_imag
    square_imag = 2.0 * green_real * green_imag
    real_part = square_real * column[0] - square_imag * column[1]
    imag_part = square_real * column[1] + square_imag * column[0]
    return COUPLING * COUPLING * jnp.stack([real_part, imag_part], axis=0)


def spread(blocks, axes):
    return lax.all_to_all(blocks, axes, 0, 0, tiled=True)


def body(green_hist, sigma_hist, prev_row, propagator, impurity_column, sigma_start):
    points, width = prev_row.shape[0], prev_row.shape[-1]
    times = lax.axis_size(TA)
    near, far = lax.axis_size(NEAR), lax.axis_size(FAR)
    point_count = points * lax.axis_size(KA)
    own_time = jnp.arange(times)[:, None] == lax.axis_index(TA)
    own_prev = jnp.where(own_time, prev_row[..., None, :], 0.0)
    own_prev = own_prev.reshape(points, 2, 2, 2, times * width)
    green_row = prev_row
    self_energy = sigma_start
    for iteration in range(ITERS):
        block = sigma_block(self_energy).astype(jnp.bfloat16)
        partial_terms = jnp.einsum(
            "oarbs,krbcst->koact", block, green_hist, preferred_element_type=jnp.float32
        )
        rows_low = row_block(green_row).astype(jnp.bfloat16)
        partial_terms = partial_terms + jnp.einsum(
            "koarbs,rbcst->koact", rows_low, sigma_hist, preferred_element_type=jnp.float32
        )
        share = propagate(propagator, own_prev + TIME_STEP * partial_terms)
        share = share.reshape(points * 8, times, width).transpose(1, 0, 2)
        share = jnp.broadcast_to(share[None], (near, times, points * 8, width))
        got = spread(share.reshape(near * times, points * 8, width), NEAR + TA)
        got = got.reshape(near, times, points, 8, width)
        own = lax.dynamic_index_in_dim(got, lax.axis_index(NEAR), 0, keepdims=False)
        green_row = jnp.sum(own, axis=0).reshape(points, 2, 2, 2, width)
        near_sum = jnp.sum(got, axis=(0, 1, 2))
        sums = spread(jnp.broadcast_to(near_sum[None], (far, 8, width)), FAR)
        local_green = (jnp.sum(sums, axis=0) / point_count).reshape(2, 2, 2, width)
        self_energy = second_order(local_green, impurity_column)
    return (green_row, self_energy)


def solution(mesh):
    fine = Mesh(mesh.devices.reshape([n for _, n in CUT]), [name for name, _ in CUT])
    placed = (
        P(KA, None, None, None, TA, None),
        P(None, None, None, TA, None),
        P(KA, None, None, None, TA),
        P(KA, None, None, None),
        P(None, None, None, TA),
        P(None, None, None, TA),
    )
    return jax.shard_map(
        body,
        mesh=fine,
        in_specs=placed,
        out_specs=(P(KA, None, None, None, TA), P(None, None, None, TA)),
        check_vma=False,
    )
```

```python
import functools

import jax
import jax.numpy as jnp
from jax import lax
from jax.experimental import pallas as pl
from jax.experimental.pallas import tpu as pltpu
from jax.sharding import Mesh, PartitionSpec as P

ITERS = 2


TIME_STEP = 0.02
COUPLING = 1.0

CUT = (("yh", 4), ("yl", 2), ("xh", 2), ("z", 8), ("xl", 2), ("core", 2))
KA = ("yh", "yl", "xh", "z")
TA = ("xl", "core")
NEAR = ("yl", "xh")
FAR = ("yh", "z")


def second_order(local_green, column):
    green_real = local_green[0]
    green_imag = local_green[1]
    square_real = green_real * green_real - green_imag * green_imag
    square_imag = 2.0 * green_real * green_imag
    real_part = square_real * column[0] - square_imag * column[1]
    imag_part = square_real * column[1] + square_imag * column[0]
    return COUPLING * COUPLING * jnp.stack([real_part, imag_part], axis=0)


def spread(blocks, axes):
    return lax.all_to_all(blocks, axes, 0, 0, tiled=True)


def parts_of(ref, index, o, r, b):
    part = ref[(*index, pl.ds(b, 1), slice(None))]
    return -part if (o == 0 and r == 1) else part


def fill_left(sigma_ref, row_ref, sigma_lhs, row_lhs):
    points, width = row_ref.shape[0], row_ref.shape[-1]
    sigma_lhs[...] = jnp.zeros_like(sigma_lhs)
    row_lhs[...] = jnp.zeros_like(row_lhs)
    for o in range(2):
        for a in range(2):
            for j in range(4):
                r, b = j // 2, j % 2
                lanes = pl.ds(j * width, width)
                part = parts_of(sigma_ref, (o ^ r, a), o, r, b)
                for c in range(2):
                    sigma_lhs[c, pl.ds(c * 4 + o * 2 + a, 1), lanes] = part
                for k in range(points):
                    part = parts_of(row_ref, (k, o ^ r, a), o, r, b)
                    for c in range(2):
                        row_lhs[c, pl.ds(k * 8 + c * 4 + o * 2 + a, 1), lanes] = part


def contract(left, blocks):
    total = None
    for c in range(2):
        right = jnp.concatenate([blocks[j][c] for j in range(4)], axis=0)
        term = jnp.dot(left[c].astype(jnp.bfloat16), right, preferred_element_type=jnp.float32)
        total = term if total is None else total + term
    return total


def propagate_share(near, times, k, inner, prev, factors, out_ref):
    width = prev.shape[-1]
    place = lax.broadcasted_iota(jnp.int32, (8, width), 0)
    own_time = lax.axis_index(TA)
    for t in range(times):
        part = TIME_STEP * inner[:, t * width:(t + 1) * width]
        part = part + jnp.where(own_time == t, prev, 0.0)
        share = None
        for j in range(4):
            low = jnp.broadcast_to(part[j:j + 1], (8, width))
            high = jnp.broadcast_to(part[4 + j:5 + j], (8, width))
            term = factors[j] * jnp.where(place < 4, low, high)
            share = term if share is None else share + term
        for n in range(near):
            for c in range(2):
                out_ref[n * times + t, pl.ds(k * 8 + c, 4, stride=2), :] = share[c * 4:(c + 1) * 4]


def first_kernel(
    near, times,
    prop_in, sigma_in, prev_in, green_in, hist_in,
    out_ref, factor_ref, own_prev, green_buf, hist_buf,
    prop_ref, sigma_ref, prev_ref, sigma_lhs, row_lhs, small, sems,
):
    points, width = prev_ref.shape[0], prev_ref.shape[-1]
    little = [
        pltpu.make_async_copy(src, dst, small.at[i])
        for i, (src, dst) in enumerate(((sigma_in, sigma_ref), (prev_in, prev_ref), (prop_in, prop_ref)))
    ]
    for copy in little:
        copy.start()
    large = {}
    for j in range(4):
        large[points, j] = pltpu.make_async_copy(hist_in.at[j // 2, j % 2], hist_buf.at[j], sems.at[points, j])
        large[points, j].start()
    for k in range(points):
        for j in range(4):
            large[k, j] = pltpu.make_async_copy(green_in.at[k, j // 2, j % 2], green_buf.at[k, j], sems.at[k, j])
            large[k, j].start()
    for copy in little:
        copy.wait()
    fill_left(sigma_ref, prev_ref, sigma_lhs, row_lhs)
    for k in range(points):
        for o in range(2):
            for a in range(2):
                for c in range(2):
                    own_prev[pl.ds(k * 8 + c * 4 + o * 2 + a, 1), :] = prev_ref[k, o, a, pl.ds(c, 1), :]
    for k in range(points):
        for r in range(2):
            for a in range(2):
                for b in range(2):
                    entry = jnp.broadcast_to(prop_ref[k, r, pl.ds(a, 1), pl.ds(b, 1)], (1, width))
                    for o in range(2):
                        value = -entry if (o == 1 and r == 1) else entry
                        for c in range(2):
                            factor_ref[k, o * 2 + b, pl.ds(c * 4 + (o ^ r) * 2 + a, 1), :] = value
    for j in range(4):
        large[points, j].wait()
    row_terms = contract(row_lhs, [[hist_buf[j, c] for c in range(2)] for j in range(4)])
    for k in range(points):
        for j in range(4):
            large[k, j].wait()
        inner = contract(sigma_lhs, [[green_buf[k, j, c] for c in range(2)] for j in range(4)])
        inner = inner + row_terms[k * 8:(k + 1) * 8]
        factors = [factor_ref[k, j] for j in range(4)]
        propagate_share(near, times, k, inner, own_prev[pl.ds(k * 8, 8), :], factors, out_ref)


def next_kernel(
    near, times,
    sigma_ref, row_ref, factor_ref, own_prev, green_ref, hist_ref, out_ref,
    sigma_lhs, row_lhs,
):
    points = row_ref.shape[0]
    fill_left(sigma_ref, row_ref, sigma_lhs, row_lhs)
    row_terms = contract(row_lhs, [[hist_ref[j, c] for c in range(2)] for j in range(4)])
    for k in range(points):
        inner = contract(sigma_lhs, [[green_ref[k, j, c] for c in range(2)] for j in range(4)])
        inner = inner + row_terms[k * 8:(k + 1) * 8]
        factors = [factor_ref[k, j] for j in range(4)]
        propagate_share(near, times, k, inner, own_prev[pl.ds(k * 8, 8), :], factors, out_ref)


VMEM = pl.BlockSpec(memory_space=pltpu.VMEM)
HBM = pl.BlockSpec(memory_space=pltpu.HBM)


def left_scratch(points, width):
    return [
        pltpu.VMEM((2, 8, 4 * width), jnp.float32),
        pltpu.VMEM((2, points * 8, 4 * width), jnp.float32),
    ]


def first_share(propagator, self_energy, prev_row, green_hist, sigma_hist, near, times):
    points, width = prev_row.shape[0], prev_row.shape[-1]
    full = sigma_hist.shape[-1]
    return pl.pallas_call(
        functools.partial(first_kernel, near, times),
        out_shape=(
            jax.ShapeDtypeStruct((near * times, points * 8, width), jnp.float32),
            jax.ShapeDtypeStruct((points, 4, 8, width), jnp.float32),
            jax.ShapeDtypeStruct((points * 8, width), jnp.float32),
            jax.ShapeDtypeStruct((points, 4, 2, width, full), jnp.bfloat16),
            jax.ShapeDtypeStruct((4, 2, width, full), jnp.bfloat16),
        ),
        in_specs=[HBM] * 5,
        out_specs=(VMEM,) * 5,
        scratch_shapes=[
            pltpu.VMEM(propagator.shape, jnp.float32),
            pltpu.VMEM(self_energy.shape, jnp.float32),
            pltpu.VMEM(prev_row.shape, jnp.float32),
            *left_scratch(points, width),
            pltpu.SemaphoreType.DMA((3,)),
            pltpu.SemaphoreType.DMA((points + 1, 4)),
        ],
        compiler_params=pltpu.CompilerParams(vmem_limit_bytes=16 << 20),
        name="first_share",
    )(*(
        pltpu.with_memory_space_constraint(x, pltpu.HBM)
        for x in (propagator, self_energy, prev_row, green_hist, sigma_hist)
    ))


def next_share(self_energy, green_row, factors, own_prev, green_hist, sigma_hist, near, times):
    points, width = green_row.shape[0], green_row.shape[-1]
    return pl.pallas_call(
        functools.partial(next_kernel, near, times),
        out_shape=jax.ShapeDtypeStruct((near * times, points * 8, width), jnp.float32),
        in_specs=[VMEM] * 6,
        out_specs=VMEM,
        scratch_shapes=left_scratch(points, width),
        compiler_params=pltpu.CompilerParams(vmem_limit_bytes=16 << 20),
        name="next_share",
    )(self_energy, green_row, factors, own_prev, green_hist, sigma_hist)


def body(green_hist, sigma_hist, prev_row, propagator, impurity_column, sigma_start):
    points, width = prev_row.shape[0], prev_row.shape[-1]
    times = lax.axis_size(TA)
    near, far = lax.axis_size(NEAR), lax.axis_size(FAR)
    point_count = points * lax.axis_size(KA)
    place = lax.axis_index(NEAR)
    column = impurity_column
    for iteration in range(ITERS):
        if iteration == 0:
            share, factors, own_prev, green_held, hist_held = first_share(
                propagator, sigma_start, prev_row, green_hist, sigma_hist, near, times
            )
        else:
            share = next_share(
                self_energy, green_row, factors, own_prev, green_held, hist_held, near, times
            )
        share, place = lax.optimization_barrier((share, place))
        got = spread(share, NEAR + TA)
        got, column = lax.optimization_barrier((got, column))
        got = got.reshape(near, times, points, 8, width)
        own = lax.dynamic_index_in_dim(got, place, 0, keepdims=False, allow_negative_indices=False)
        green_row = jnp.sum(own, axis=0).reshape(points, 2, 2, 2, width)
        near_sum = jnp.sum(got, axis=(0, 1, 2))
        near_sum, green_row = lax.optimization_barrier((near_sum, green_row))
        sums = spread(jnp.broadcast_to(near_sum[None], (far, 8, width)), FAR)
        sums, green_row = lax.optimization_barrier((sums, green_row))
        local_green = (jnp.sum(sums, axis=0) / point_count).reshape(2, 2, 2, width)
        self_energy = second_order(local_green, column)
    return (green_row, self_energy)


def solution(mesh):
    fine = Mesh(mesh.devices.reshape([n for _, n in CUT]), [name for name, _ in CUT])
    placed = (
        P(KA, None, None, None, TA, None),
        P(None, None, None, TA, None),
        P(KA, None, None, None, TA),
        P(KA, None, None, None),
        P(None, None, None, TA),
        P(None, None, None, TA),
    )
    return jax.shard_map(
        body,
        mesh=fine,
        in_specs=placed,
        out_specs=(P(KA, None, None, None, TA), P(None, None, None, TA)),
        check_vma=False,
    )
```

```python
import functools

import jax
import jax.numpy as jnp
from jax import lax
from jax.experimental import pallas as pl
from jax.experimental.pallas import tpu as pltpu
from jax.sharding import Mesh, PartitionSpec as P

ITERS = 2


TIME_STEP = 0.02
COUPLING = 1.0

CUT = (("yh", 4), ("yl", 2), ("xh", 2), ("z", 8), ("xl", 2), ("core", 2))
KA = ("yh", "yl", "xh", "z")
TA = ("xl", "core")
NEAR = ("yl", "xh")
FAR = ("yh", "z")


def second_order(local_green, column):
    green_real = local_green[0]
    green_imag = local_green[1]
    square_real = green_real * green_real - green_imag * green_imag
    square_imag = 2.0 * green_real * green_imag
    real_part = square_real * column[0] - square_imag * column[1]
    imag_part = square_real * column[1] + square_imag * column[0]
    return COUPLING * COUPLING * real_part, COUPLING * COUPLING * imag_part


def spread(blocks, axes):
    return lax.all_to_all(blocks, axes, 0, 0, tiled=True)


def parts_of(ref, index, o, r, b):
    part = ref[(*index, pl.ds(b, 1), slice(None))]
    return -part if (o == 0 and r == 1) else part


def fill_left(sigma_ref, row_ref, sigma_lhs, row_lhs):
    points, width = row_ref.shape[0], row_ref.shape[-1]
    sigma_lhs[...] = jnp.zeros_like(sigma_lhs)
    row_lhs[...] = jnp.zeros_like(row_lhs)
    for o in range(2):
        for a in range(2):
            for j in range(4):
                r, b = j // 2, j % 2
                lanes = pl.ds(j * width, width)
                part = parts_of(sigma_ref, (o ^ r, a), o, r, b)
                for c in range(2):
                    sigma_lhs[c, pl.ds(c * 4 + o * 2 + a, 1), lanes] = part
                for k in range(points):
                    part = parts_of(row_ref, (k, o ^ r, a), o, r, b)
                    for c in range(2):
                        row_lhs[c, pl.ds(k * 8 + c * 4 + o * 2 + a, 1), lanes] = part


def contract(left, blocks):
    total = None
    for c in range(2):
        right = jnp.concatenate([blocks[j][c] for j in range(4)], axis=0)
        term = jnp.dot(left[c].astype(jnp.bfloat16), right, preferred_element_type=jnp.float32)
        total = term if total is None else total + term
    return total


def propagate_share(near, times, k, inner, prev, factors, out_ref):
    width = prev.shape[-1]
    place = lax.broadcasted_iota(jnp.int32, (8, width), 0)
    own_time = lax.axis_index(TA)
    for t in range(times):
        part = TIME_STEP * inner[:, t * width:(t + 1) * width]
        part = part + jnp.where(own_time == t, prev, 0.0)
        share = None
        for j in range(4):
            low = jnp.broadcast_to(part[j:j + 1], (8, width))
            high = jnp.broadcast_to(part[4 + j:5 + j], (8, width))
            term = factors[j] * jnp.where(place < 4, low, high)
            share = term if share is None else share + term
        for n in range(near):
            for c in range(2):
                out_ref[n * times + t, pl.ds(k * 8 + c, 4, stride=2), :] = share[c * 4:(c + 1) * 4]


def first_kernel(
    near, times,
    prop_in, sigma_in, prev_in, green_in, hist_in,
    out_ref, factor_ref, own_prev, green_buf, hist_buf,
    prop_ref, sigma_ref, prev_ref, sigma_lhs, row_lhs, small, sems,
):
    points, width = prev_ref.shape[0], prev_ref.shape[-1]
    little = [
        pltpu.make_async_copy(src, dst, small.at[i])
        for i, (src, dst) in enumerate(((sigma_in, sigma_ref), (prev_in, prev_ref), (prop_in, prop_ref)))
    ]
    for copy in little:
        copy.start()
    large = {}
    for j in range(4):
        large[points, j] = pltpu.make_async_copy(hist_in.at[j // 2, j % 2], hist_buf.at[j], sems.at[points, j])
        large[points, j].start()
    for k in range(points):
        for j in range(4):
            large[k, j] = pltpu.make_async_copy(green_in.at[k, j // 2, j % 2], green_buf.at[k, j], sems.at[k, j])
            large[k, j].start(priority=1)
    for copy in little:
        copy.wait()
    fill_left(sigma_ref, prev_ref, sigma_lhs, row_lhs)
    for k in range(points):
        for o in range(2):
            for a in range(2):
                for c in range(2):
                    own_prev[pl.ds(k * 8 + c * 4 + o * 2 + a, 1), :] = prev_ref[k, o, a, pl.ds(c, 1), :]
    for k in range(points):
        for r in range(2):
            for a in range(2):
                for b in range(2):
                    entry = jnp.broadcast_to(prop_ref[k, r, pl.ds(a, 1), pl.ds(b, 1)], (1, width))
                    for o in range(2):
                        value = -entry if (o == 1 and r == 1) else entry
                        for c in range(2):
                            factor_ref[k, o * 2 + b, pl.ds(c * 4 + (o ^ r) * 2 + a, 1), :] = value
    for j in range(4):
        large[points, j].wait()
    row_terms = contract(row_lhs, [[hist_buf[j, c] for c in range(2)] for j in range(4)])
    for k in range(points):
        for j in range(4):
            large[k, j].wait()
        inner = contract(sigma_lhs, [[green_buf[k, j, c] for c in range(2)] for j in range(4)])
        inner = inner + row_terms[k * 8:(k + 1) * 8]
        factors = [factor_ref[k, j] for j in range(4)]
        propagate_share(near, times, k, inner, own_prev[pl.ds(k * 8, 8), :], factors, out_ref)


def next_kernel(
    near, times,
    sigma_ref, row_ref, factor_ref, own_prev, green_ref, hist_ref, out_ref,
    sigma_lhs, row_lhs,
):
    points = row_ref.shape[0]
    fill_left(sigma_ref, row_ref, sigma_lhs, row_lhs)
    row_terms = contract(row_lhs, [[hist_ref[j, c] for c in range(2)] for j in range(4)])
    for k in range(points):
        inner = contract(sigma_lhs, [[green_ref[k, j, c] for c in range(2)] for j in range(4)])
        inner = inner + row_terms[k * 8:(k + 1) * 8]
        factors = [factor_ref[k, j] for j in range(4)]
        propagate_share(near, times, k, inner, own_prev[pl.ds(k * 8, 8), :], factors, out_ref)


def last_kernel(
    point_count, sums_ref, row_ref, column_ref, row_out, energy_out, energy_ref, local_ref, sems,
):
    row_copy = pltpu.make_async_copy(row_ref, row_out, sems.at[0])
    row_copy.start()
    local_ref[...] = jnp.sum(sums_ref[...], axis=0) / point_count
    for a in range(2):
        local = [local_ref[pl.ds(o * 4 + a * 2, 2), :] for o in range(2)]
        parts = second_order(local, [column_ref[o, a] for o in range(2)])
        for o in range(2):
            energy_ref[o, a] = parts[o]
    energy_copy = pltpu.make_async_copy(energy_ref, energy_out, sems.at[1])
    energy_copy.start()
    row_copy.wait()
    energy_copy.wait()


VMEM = pl.BlockSpec(memory_space=pltpu.VMEM)
HBM = pl.BlockSpec(memory_space=pltpu.HBM)


def left_scratch(points, width):
    return [
        pltpu.VMEM((2, 8, 4 * width), jnp.float32),
        pltpu.VMEM((2, points * 8, 4 * width), jnp.float32),
    ]


def first_share(propagator, self_energy, prev_row, green_hist, sigma_hist, near, times):
    points, width = prev_row.shape[0], prev_row.shape[-1]
    full = sigma_hist.shape[-1]
    return pl.pallas_call(
        functools.partial(first_kernel, near, times),
        out_shape=(
            jax.ShapeDtypeStruct((near * times, points * 8, width), jnp.float32),
            jax.ShapeDtypeStruct((points, 4, 8, width), jnp.float32),
            jax.ShapeDtypeStruct((points * 8, width), jnp.float32),
            jax.ShapeDtypeStruct((points, 4, 2, width, full), jnp.bfloat16),
            jax.ShapeDtypeStruct((4, 2, width, full), jnp.bfloat16),
        ),
        in_specs=[HBM] * 5,
        out_specs=(VMEM,) * 5,
        scratch_shapes=[
            pltpu.VMEM(propagator.shape, jnp.float32),
            pltpu.VMEM(self_energy.shape, jnp.float32),
            pltpu.VMEM(prev_row.shape, jnp.float32),
            *left_scratch(points, width),
            pltpu.SemaphoreType.DMA((3,)),
            pltpu.SemaphoreType.DMA((points + 1, 4)),
        ],
        compiler_params=pltpu.CompilerParams(vmem_limit_bytes=16 << 20),
        name="first_share",
    )(*(
        pltpu.with_memory_space_constraint(x, pltpu.HBM)
        for x in (propagator, self_energy, prev_row, green_hist, sigma_hist)
    ))


def next_share(self_energy, green_row, factors, own_prev, green_hist, sigma_hist, near, times):
    points, width = green_row.shape[0], green_row.shape[-1]
    return pl.pallas_call(
        functools.partial(next_kernel, near, times),
        out_shape=jax.ShapeDtypeStruct((near * times, points * 8, width), jnp.float32),
        in_specs=[VMEM] * 6,
        out_specs=VMEM,
        scratch_shapes=left_scratch(points, width),
        compiler_params=pltpu.CompilerParams(vmem_limit_bytes=16 << 20),
        name="next_share",
    )(self_energy, green_row, factors, own_prev, green_hist, sigma_hist)


def last_step(sums, green_row, column, point_count):
    return pl.pallas_call(
        functools.partial(last_kernel, point_count),
        out_shape=(
            jax.ShapeDtypeStruct(green_row.shape, jnp.float32),
            jax.ShapeDtypeStruct(column.shape, jnp.float32),
        ),
        in_specs=[VMEM] * 3,
        out_specs=(HBM,) * 2,
        scratch_shapes=[
            pltpu.VMEM(column.shape, jnp.float32),
            pltpu.VMEM(sums.shape[1:], jnp.float32),
            pltpu.SemaphoreType.DMA((2,)),
        ],
        compiler_params=pltpu.CompilerParams(vmem_limit_bytes=16 << 20),
        name="last_step",
    )(sums, green_row, column)


def body(green_hist, sigma_hist, prev_row, propagator, impurity_column, sigma_start):
    points, width = prev_row.shape[0], prev_row.shape[-1]
    times = lax.axis_size(TA)
    near, far = lax.axis_size(NEAR), lax.axis_size(FAR)
    point_count = points * lax.axis_size(KA)
    place = lax.axis_index(NEAR)
    column = impurity_column
    for iteration in range(ITERS):
        if iteration == 0:
            share, factors, own_prev, green_held, hist_held = first_share(
                propagator, sigma_start, prev_row, green_hist, sigma_hist, near, times
            )
        else:
            share = next_share(
                self_energy, green_row, factors, own_prev, green_held, hist_held, near, times
            )
        share, place = lax.optimization_barrier((share, place))
        got = spread(share, NEAR + TA)
        got, column = lax.optimization_barrier((got, column))
        got = got.reshape(near, times, points, 8, width)
        own = lax.dynamic_index_in_dim(got, place, 0, keepdims=False, allow_negative_indices=False)
        green_row = jnp.sum(own, axis=0).reshape(points, 2, 2, 2, width)
        near_sum = jnp.sum(got, axis=(0, 1, 2))
        near_sum, green_row = lax.optimization_barrier((near_sum, green_row))
        sums = spread(jnp.broadcast_to(near_sum[None], (far, 8, width)), FAR)
        sums, green_row = lax.optimization_barrier((sums, green_row))
        if iteration == ITERS - 1:
            return last_step(sums, green_row, column, point_count)
        local_green = (jnp.sum(sums, axis=0) / point_count).reshape(2, 2, 2, width)
        self_energy = jnp.stack(second_order(local_green, column), axis=0)


def solution(mesh):
    fine = Mesh(mesh.devices.reshape([n for _, n in CUT]), [name for name, _ in CUT])
    placed = (
        P(KA, None, None, None, TA, None),
        P(None, None, None, TA, None),
        P(KA, None, None, None, TA),
        P(KA, None, None, None),
        P(None, None, None, TA),
        P(None, None, None, TA),
    )
    return jax.shard_map(
        body,
        mesh=fine,
        in_specs=placed,
        out_specs=(P(KA, None, None, None, TA), P(None, None, None, TA)),
        check_vma=False,
    )
```

```python
import functools

import jax
import jax.numpy as jnp
from jax import lax
from jax.experimental import pallas as pl
from jax.experimental.pallas import tpu as pltpu
from jax.sharding import Mesh, PartitionSpec as P

ITERS = 2


TIME_STEP = 0.02
COUPLING = 1.0

CUT = (("yh", 4), ("yl", 2), ("xh", 2), ("z", 8), ("xl", 2), ("core", 2))
KA = ("yh", "yl", "xh", "z")
TA = ("xl", "core")
NEAR = ("yl", "xh")
FAR = ("yh", "z")
NEAR_FIRST = (0, 0)
FAR_FIRST = (22, 22)


def second_order(local_green, column):
    green_real = local_green[0]
    green_imag = local_green[1]
    square_real = green_real * green_real - green_imag * green_imag
    square_imag = 2.0 * green_real * green_imag
    real_part = square_real * column[0] - square_imag * column[1]
    imag_part = square_real * column[1] + square_imag * column[0]
    return COUPLING * COUPLING * real_part, COUPLING * COUPLING * imag_part


def spread(blocks, axes, first):
    order = [rank ^ first for rank in range(lax.axis_size(axes))]
    return lax.all_to_all(blocks, axes, 0, 0, tiled=True, axis_index_groups=[order])


def parts_of(ref, index, o, r, b):
    part = ref[(*index, pl.ds(b, 1), slice(None))]
    return -part if (o == 0 and r == 1) else part


def fill_left(sigma_ref, row_ref, sigma_lhs, row_lhs):
    points, width = row_ref.shape[0], row_ref.shape[-1]
    sigma_lhs[...] = jnp.zeros_like(sigma_lhs)
    row_lhs[...] = jnp.zeros_like(row_lhs)
    for o in range(2):
        for a in range(2):
            for j in range(4):
                r, b = j // 2, j % 2
                lanes = pl.ds(j * width, width)
                part = parts_of(sigma_ref, (o ^ r, a), o, r, b)
                for c in range(2):
                    sigma_lhs[c, pl.ds(c * 4 + o * 2 + a, 1), lanes] = part
                for k in range(points):
                    part = parts_of(row_ref, (k, o ^ r, a), o, r, b)
                    for c in range(2):
                        row_lhs[c, pl.ds(k * 8 + c * 4 + o * 2 + a, 1), lanes] = part


def contract(left, blocks):
    total = None
    for c in range(2):
        right = jnp.concatenate([blocks[j][c] for j in range(4)], axis=0)
        term = jnp.dot(left[c].astype(jnp.bfloat16), right, preferred_element_type=jnp.float32)
        total = term if total is None else total + term
    return total


def propagate_share(near, times, first, k, inner, prev, factors, out_ref):
    width = prev.shape[-1]
    place = lax.broadcasted_iota(jnp.int32, (8, width), 0)
    own_time = lax.axis_index(TA)
    for t in range(times):
        part = TIME_STEP * inner[:, t * width:(t + 1) * width]
        part = part + jnp.where(own_time == t, prev, 0.0)
        share = None
        for j in range(4):
            low = jnp.broadcast_to(part[j:j + 1], (8, width))
            high = jnp.broadcast_to(part[4 + j:5 + j], (8, width))
            term = factors[j] * jnp.where(place < 4, low, high)
            share = term if share is None else share + term
        for n in range(near):
            for c in range(2):
                out_ref[n * times + (t ^ first), pl.ds(k * 8 + c, 4, stride=2), :] = share[c * 4:(c + 1) * 4]


def first_kernel(
    near, times, first,
    prop_in, sigma_in, prev_in, green_in, hist_in,
    out_ref, factor_ref, own_prev, green_buf, hist_buf,
    prop_ref, sigma_ref, prev_ref, sigma_lhs, row_lhs, small, sems,
):
    points, width = prev_ref.shape[0], prev_ref.shape[-1]
    little = [
        pltpu.make_async_copy(src, dst, small.at[i])
        for i, (src, dst) in enumerate(((sigma_in, sigma_ref), (prev_in, prev_ref), (prop_in, prop_ref)))
    ]
    for copy in little:
        copy.start()
    large = {}
    for j in range(4):
        large[points, j] = pltpu.make_async_copy(hist_in.at[j // 2, j % 2], hist_buf.at[j], sems.at[points, j])
        large[points, j].start()
    for k in range(points):
        for j in range(4):
            large[k, j] = pltpu.make_async_copy(green_in.at[k, j // 2, j % 2], green_buf.at[k, j], sems.at[k, j])
            large[k, j].start(priority=1)
    for copy in little:
        copy.wait()
    fill_left(sigma_ref, prev_ref, sigma_lhs, row_lhs)
    for k in range(points):
        for o in range(2):
            for a in range(2):
                for c in range(2):
                    own_prev[pl.ds(k * 8 + c * 4 + o * 2 + a, 1), :] = prev_ref[k, o, a, pl.ds(c, 1), :]
    for k in range(points):
        for r in range(2):
            for a in range(2):
                for b in range(2):
                    entry = jnp.broadcast_to(prop_ref[k, r, pl.ds(a, 1), pl.ds(b, 1)], (1, width))
                    for o in range(2):
                        value = -entry if (o == 1 and r == 1) else entry
                        for c in range(2):
                            factor_ref[k, o * 2 + b, pl.ds(c * 4 + (o ^ r) * 2 + a, 1), :] = value
    for j in range(4):
        large[points, j].wait()
    row_terms = contract(row_lhs, [[hist_buf[j, c] for c in range(2)] for j in range(4)])
    for k in range(points):
        for j in range(4):
            large[k, j].wait()
        inner = contract(sigma_lhs, [[green_buf[k, j, c] for c in range(2)] for j in range(4)])
        inner = inner + row_terms[k * 8:(k + 1) * 8]
        factors = [factor_ref[k, j] for j in range(4)]
        propagate_share(near, times, first, k, inner, own_prev[pl.ds(k * 8, 8), :], factors, out_ref)


def next_kernel(
    near, times, first,
    sigma_ref, row_ref, factor_ref, own_prev, green_ref, hist_ref, out_ref,
    sigma_lhs, row_lhs,
):
    points = row_ref.shape[0]
    fill_left(sigma_ref, row_ref, sigma_lhs, row_lhs)
    row_terms = contract(row_lhs, [[hist_ref[j, c] for c in range(2)] for j in range(4)])
    for k in range(points):
        inner = contract(sigma_lhs, [[green_ref[k, j, c] for c in range(2)] for j in range(4)])
        inner = inner + row_terms[k * 8:(k + 1) * 8]
        factors = [factor_ref[k, j] for j in range(4)]
        propagate_share(near, times, first, k, inner, own_prev[pl.ds(k * 8, 8), :], factors, out_ref)


def last_kernel(
    point_count, sums_ref, row_ref, column_ref, row_out, energy_out, energy_ref, local_ref, sems,
):
    row_copy = pltpu.make_async_copy(row_ref, row_out, sems.at[0])
    row_copy.start()
    local_ref[...] = jnp.sum(sums_ref[...], axis=0) / point_count
    for a in range(2):
        local = [local_ref[pl.ds(o * 4 + a * 2, 2), :] for o in range(2)]
        parts = second_order(local, [column_ref[o, a] for o in range(2)])
        for o in range(2):
            energy_ref[o, a] = parts[o]
    energy_copy = pltpu.make_async_copy(energy_ref, energy_out, sems.at[1])
    energy_copy.start()
    row_copy.wait()
    energy_copy.wait()


VMEM = pl.BlockSpec(memory_space=pltpu.VMEM)
HBM = pl.BlockSpec(memory_space=pltpu.HBM)


def left_scratch(points, width):
    return [
        pltpu.VMEM((2, 8, 4 * width), jnp.float32),
        pltpu.VMEM((2, points * 8, 4 * width), jnp.float32),
    ]


def first_share(propagator, self_energy, prev_row, green_hist, sigma_hist, near, times, first):
    points, width = prev_row.shape[0], prev_row.shape[-1]
    full = sigma_hist.shape[-1]
    return pl.pallas_call(
        functools.partial(first_kernel, near, times, first),
        out_shape=(
            jax.ShapeDtypeStruct((near * times, points * 8, width), jnp.float32),
            jax.ShapeDtypeStruct((points, 4, 8, width), jnp.float32),
            jax.ShapeDtypeStruct((points * 8, width), jnp.float32),
            jax.ShapeDtypeStruct((points, 4, 2, width, full), jnp.bfloat16),
            jax.ShapeDtypeStruct((4, 2, width, full), jnp.bfloat16),
        ),
        in_specs=[HBM] * 5,
        out_specs=(VMEM,) * 5,
        scratch_shapes=[
            pltpu.VMEM(propagator.shape, jnp.float32),
            pltpu.VMEM(self_energy.shape, jnp.float32),
            pltpu.VMEM(prev_row.shape, jnp.float32),
            *left_scratch(points, width),
            pltpu.SemaphoreType.DMA((3,)),
            pltpu.SemaphoreType.DMA((points + 1, 4)),
        ],
        compiler_params=pltpu.CompilerParams(vmem_limit_bytes=16 << 20),
        name="first_share",
    )(*(
        pltpu.with_memory_space_constraint(x, pltpu.HBM)
        for x in (propagator, self_energy, prev_row, green_hist, sigma_hist)
    ))


def next_share(self_energy, green_row, factors, own_prev, green_hist, sigma_hist, near, times, first):
    points, width = green_row.shape[0], green_row.shape[-1]
    return pl.pallas_call(
        functools.partial(next_kernel, near, times, first),
        out_shape=jax.ShapeDtypeStruct((near * times, points * 8, width), jnp.float32),
        in_specs=[VMEM] * 6,
        out_specs=VMEM,
        scratch_shapes=left_scratch(points, width),
        compiler_params=pltpu.CompilerParams(vmem_limit_bytes=16 << 20),
        name="next_share",
    )(self_energy, green_row, factors, own_prev, green_hist, sigma_hist)


def last_step(sums, green_row, column, point_count):
    return pl.pallas_call(
        functools.partial(last_kernel, point_count),
        out_shape=(
            jax.ShapeDtypeStruct(green_row.shape, jnp.float32),
            jax.ShapeDtypeStruct(column.shape, jnp.float32),
        ),
        in_specs=[VMEM] * 3,
        out_specs=(HBM,) * 2,
        scratch_shapes=[
            pltpu.VMEM(column.shape, jnp.float32),
            pltpu.VMEM(sums.shape[1:], jnp.float32),
            pltpu.SemaphoreType.DMA((2,)),
        ],
        compiler_params=pltpu.CompilerParams(vmem_limit_bytes=16 << 20),
        name="last_step",
    )(sums, green_row, column)


def body(green_hist, sigma_hist, prev_row, propagator, impurity_column, sigma_start):
    points, width = prev_row.shape[0], prev_row.shape[-1]
    times = lax.axis_size(TA)
    near, far = lax.axis_size(NEAR), lax.axis_size(FAR)
    point_count = points * lax.axis_size(KA)
    place = lax.axis_index(NEAR)
    column = impurity_column
    for iteration in range(ITERS):
        first = NEAR_FIRST[iteration] % times
        if iteration == 0:
            share, factors, own_prev, green_held, hist_held = first_share(
                propagator, sigma_start, prev_row, green_hist, sigma_hist, near, times, first
            )
        else:
            share = next_share(
                self_energy, green_row, factors, own_prev, green_held, hist_held, near, times, first
            )
        share, place = lax.optimization_barrier((share, place))
        got = spread(share, NEAR + TA, NEAR_FIRST[iteration])
        got, column = lax.optimization_barrier((got, column))
        got = got.reshape(near, times, points, 8, width)
        own = lax.dynamic_index_in_dim(got, place ^ (NEAR_FIRST[iteration] // times), 0, keepdims=False, allow_negative_indices=False)
        green_row = jnp.sum(own, axis=0).reshape(points, 2, 2, 2, width)
        near_sum = jnp.sum(got, axis=(0, 1, 2))
        near_sum, green_row = lax.optimization_barrier((near_sum, green_row))
        sums = spread(jnp.broadcast_to(near_sum[None], (far, 8, width)), FAR, FAR_FIRST[iteration])
        sums, green_row = lax.optimization_barrier((sums, green_row))
        if iteration == ITERS - 1:
            return last_step(sums, green_row, column, point_count)
        local_green = (jnp.sum(sums, axis=0) / point_count).reshape(2, 2, 2, width)
        self_energy = jnp.stack(second_order(local_green, column), axis=0)


def solution(mesh):
    fine = Mesh(mesh.devices.reshape([n for _, n in CUT]), [name for name, _ in CUT])
    placed = (
        P(KA, None, None, None, TA, None),
        P(None, None, None, TA, None),
        P(KA, None, None, None, TA),
        P(KA, None, None, None),
        P(None, None, None, TA),
        P(None, None, None, TA),
    )
    return jax.shard_map(
        body,
        mesh=fine,
        in_specs=placed,
        out_specs=(P(KA, None, None, None, TA), P(None, None, None, TA)),
        check_vma=False,
    )
```

```python
import functools

import jax
import jax.numpy as jnp
from jax import lax
from jax.experimental import pallas as pl
from jax.experimental.pallas import tpu as pltpu
from jax.sharding import Mesh, PartitionSpec as P

ITERS = 2


TIME_STEP = 0.02
COUPLING = 1.0

CUT = (("yh", 4), ("yl", 2), ("xh", 2), ("z", 8), ("xl", 2), ("core", 2))
KA = ("yh", "yl", "xh", "z")
TA = ("xl", "core")
NEAR = ("yl", "xh")
FAR = ("yh", "z")
NEAR_FIRST = (13, 13)
FAR_FIRST = (21, 21)


def second_order(local_green, column):
    green_real = local_green[0]
    green_imag = local_green[1]
    square_real = green_real * green_real - green_imag * green_imag
    square_imag = 2.0 * green_real * green_imag
    real_part = square_real * column[0] - square_imag * column[1]
    imag_part = square_real * column[1] + square_imag * column[0]
    return COUPLING * COUPLING * real_part, COUPLING * COUPLING * imag_part


def spread(blocks, axes, first):
    order = [rank ^ first for rank in range(lax.axis_size(axes))]
    return lax.all_to_all(blocks, axes, 0, 0, tiled=True, axis_index_groups=[order])


def parts_of(ref, index, o, r, b):
    part = ref[(*index, pl.ds(b, 1), slice(None))]
    return -part if (o == 0 and r == 1) else part


def fill_left(sigma_ref, row_ref, sigma_lhs, row_lhs):
    points, width = row_ref.shape[0], row_ref.shape[-1]
    sigma_lhs[...] = jnp.zeros_like(sigma_lhs)
    row_lhs[...] = jnp.zeros_like(row_lhs)
    for o in range(2):
        for a in range(2):
            for j in range(4):
                r, b = j // 2, j % 2
                lanes = pl.ds(j * width, width)
                part = parts_of(sigma_ref, (o ^ r, a), o, r, b)
                for c in range(2):
                    sigma_lhs[c, pl.ds(c * 4 + o * 2 + a, 1), lanes] = part
                for k in range(points):
                    part = parts_of(row_ref, (k, o ^ r, a), o, r, b)
                    for c in range(2):
                        row_lhs[c, pl.ds(k * 8 + c * 4 + o * 2 + a, 1), lanes] = part


def contract(left, blocks):
    total = None
    for c in range(2):
        right = jnp.concatenate([blocks[j][c] for j in range(4)], axis=0)
        term = jnp.dot(left[c].astype(jnp.bfloat16), right, preferred_element_type=jnp.float32)
        total = term if total is None else total + term
    return total


def propagate_share(near, times, first, k, inner, prev, factors, out_ref):
    width = prev.shape[-1]
    place = lax.broadcasted_iota(jnp.int32, (8, width), 0)
    own_time = lax.axis_index(TA)
    for t in range(times):
        part = TIME_STEP * inner[:, t * width:(t + 1) * width]
        part = part + jnp.where(own_time == t, prev, 0.0)
        share = None
        for j in range(4):
            low = jnp.broadcast_to(part[j:j + 1], (8, width))
            high = jnp.broadcast_to(part[4 + j:5 + j], (8, width))
            term = factors[j] * jnp.where(place < 4, low, high)
            share = term if share is None else share + term
        for n in range(near):
            for c in range(2):
                out_ref[n * times + (t ^ first), pl.ds(k * 8 + c, 4, stride=2), :] = share[c * 4:(c + 1) * 4]


def first_kernel(
    near, times, first,
    prop_in, sigma_in, prev_in, green_in, hist_in,
    out_ref, factor_ref, own_prev, green_buf, hist_buf,
    prop_ref, sigma_ref, prev_ref, sigma_lhs, row_lhs, small, sems,
):
    points, width = prev_ref.shape[0], prev_ref.shape[-1]
    little = [
        pltpu.make_async_copy(src, dst, small.at[i])
        for i, (src, dst) in enumerate(((sigma_in, sigma_ref), (prev_in, prev_ref), (prop_in, prop_ref)))
    ]
    for copy in little:
        copy.start()
    large = {}
    for j in range(4):
        large[points, j] = pltpu.make_async_copy(hist_in.at[j // 2, j % 2], hist_buf.at[j], sems.at[points, j])
        large[points, j].start()
    for k in range(points):
        for j in range(4):
            large[k, j] = pltpu.make_async_copy(green_in.at[k, j // 2, j % 2], green_buf.at[k, j], sems.at[k, j])
            large[k, j].start(priority=1)
    for copy in little:
        copy.wait()
    fill_left(sigma_ref, prev_ref, sigma_lhs, row_lhs)
    for k in range(points):
        for o in range(2):
            for a in range(2):
                for c in range(2):
                    own_prev[pl.ds(k * 8 + c * 4 + o * 2 + a, 1), :] = prev_ref[k, o, a, pl.ds(c, 1), :]
    for k in range(points):
        for r in range(2):
            for a in range(2):
                for b in range(2):
                    entry = jnp.broadcast_to(prop_ref[k, r, pl.ds(a, 1), pl.ds(b, 1)], (1, width))
                    for o in range(2):
                        value = -entry if (o == 1 and r == 1) else entry
                        for c in range(2):
                            factor_ref[k, o * 2 + b, pl.ds(c * 4 + (o ^ r) * 2 + a, 1), :] = value
    for j in range(4):
        large[points, j].wait()
    row_terms = contract(row_lhs, [[hist_buf[j, c] for c in range(2)] for j in range(4)])
    for k in range(points):
        for j in range(4):
            large[k, j].wait()
        inner = contract(sigma_lhs, [[green_buf[k, j, c] for c in range(2)] for j in range(4)])
        inner = inner + row_terms[k * 8:(k + 1) * 8]
        factors = [factor_ref[k, j] for j in range(4)]
        propagate_share(near, times, first, k, inner, own_prev[pl.ds(k * 8, 8), :], factors, out_ref)


def next_kernel(
    near, times, first,
    sigma_ref, row_ref, factor_ref, own_prev, green_ref, hist_ref, out_ref,
    sigma_lhs, row_lhs,
):
    points = row_ref.shape[0]
    fill_left(sigma_ref, row_ref, sigma_lhs, row_lhs)
    row_terms = contract(row_lhs, [[hist_ref[j, c] for c in range(2)] for j in range(4)])
    for k in range(points):
        inner = contract(sigma_lhs, [[green_ref[k, j, c] for c in range(2)] for j in range(4)])
        inner = inner + row_terms[k * 8:(k + 1) * 8]
        factors = [factor_ref[k, j] for j in range(4)]
        propagate_share(near, times, first, k, inner, own_prev[pl.ds(k * 8, 8), :], factors, out_ref)


def last_kernel(
    point_count, sums_ref, row_ref, column_ref, row_out, energy_out, energy_ref, local_ref, sems,
):
    row_copy = pltpu.make_async_copy(row_ref, row_out, sems.at[0])
    row_copy.start()
    local_ref[...] = jnp.sum(sums_ref[...], axis=0) / point_count
    for a in range(2):
        local = [local_ref[pl.ds(o * 4 + a * 2, 2), :] for o in range(2)]
        parts = second_order(local, [column_ref[o, a] for o in range(2)])
        for o in range(2):
            energy_ref[o, a] = parts[o]
    energy_copy = pltpu.make_async_copy(energy_ref, energy_out, sems.at[1])
    energy_copy.start()
    row_copy.wait()
    energy_copy.wait()


VMEM = pl.BlockSpec(memory_space=pltpu.VMEM)
HBM = pl.BlockSpec(memory_space=pltpu.HBM)


def left_scratch(points, width):
    return [
        pltpu.VMEM((2, 8, 4 * width), jnp.float32),
        pltpu.VMEM((2, points * 8, 4 * width), jnp.float32),
    ]


def first_share(propagator, self_energy, prev_row, green_hist, sigma_hist, near, times, first):
    points, width = prev_row.shape[0], prev_row.shape[-1]
    full = sigma_hist.shape[-1]
    return pl.pallas_call(
        functools.partial(first_kernel, near, times, first),
        out_shape=(
            jax.ShapeDtypeStruct((near * times, points * 8, width), jnp.float32),
            jax.ShapeDtypeStruct((points, 4, 8, width), jnp.float32),
            jax.ShapeDtypeStruct((points * 8, width), jnp.float32),
            jax.ShapeDtypeStruct((points, 4, 2, width, full), jnp.bfloat16),
            jax.ShapeDtypeStruct((4, 2, width, full), jnp.bfloat16),
        ),
        in_specs=[HBM] * 5,
        out_specs=(VMEM,) * 5,
        scratch_shapes=[
            pltpu.VMEM(propagator.shape, jnp.float32),
            pltpu.VMEM(self_energy.shape, jnp.float32),
            pltpu.VMEM(prev_row.shape, jnp.float32),
            *left_scratch(points, width),
            pltpu.SemaphoreType.DMA((3,)),
            pltpu.SemaphoreType.DMA((points + 1, 4)),
        ],
        compiler_params=pltpu.CompilerParams(vmem_limit_bytes=16 << 20),
        name="first_share",
    )(*(
        pltpu.with_memory_space_constraint(x, pltpu.HBM)
        for x in (propagator, self_energy, prev_row, green_hist, sigma_hist)
    ))


def next_share(self_energy, green_row, factors, own_prev, green_hist, sigma_hist, near, times, first):
    points, width = green_row.shape[0], green_row.shape[-1]
    return pl.pallas_call(
        functools.partial(next_kernel, near, times, first),
        out_shape=jax.ShapeDtypeStruct((near * times, points * 8, width), jnp.float32),
        in_specs=[VMEM] * 6,
        out_specs=VMEM,
        scratch_shapes=left_scratch(points, width),
        compiler_params=pltpu.CompilerParams(vmem_limit_bytes=16 << 20),
        name="next_share",
    )(self_energy, green_row, factors, own_prev, green_hist, sigma_hist)


def last_step(sums, green_row, column, point_count):
    return pl.pallas_call(
        functools.partial(last_kernel, point_count),
        out_shape=(
            jax.ShapeDtypeStruct(green_row.shape, jnp.float32),
            jax.ShapeDtypeStruct(column.shape, jnp.float32),
        ),
        in_specs=[VMEM] * 3,
        out_specs=(HBM,) * 2,
        scratch_shapes=[
            pltpu.VMEM(column.shape, jnp.float32),
            pltpu.VMEM(sums.shape[1:], jnp.float32),
            pltpu.SemaphoreType.DMA((2,)),
        ],
        compiler_params=pltpu.CompilerParams(vmem_limit_bytes=16 << 20),
        name="last_step",
    )(sums, green_row, column)


def body(green_hist, sigma_hist, prev_row, propagator, impurity_column, sigma_start):
    points, width = prev_row.shape[0], prev_row.shape[-1]
    times = lax.axis_size(TA)
    near, far = lax.axis_size(NEAR), lax.axis_size(FAR)
    point_count = points * lax.axis_size(KA)
    places = [lax.axis_index(NEAR) ^ (first // times) for first in NEAR_FIRST]
    column = impurity_column
    for iteration in range(ITERS):
        first = NEAR_FIRST[iteration] % times
        if iteration == 0:
            share, factors, own_prev, green_held, hist_held = first_share(
                propagator, sigma_start, prev_row, green_hist, sigma_hist, near, times, first
            )
        else:
            share = next_share(
                self_energy, green_row, factors, own_prev, green_held, hist_held, near, times, first
            )
        share, *places = lax.optimization_barrier((share, *places))
        got = spread(share, NEAR + TA, NEAR_FIRST[iteration])
        got, column = lax.optimization_barrier((got, column))
        got = got.reshape(near, times, points, 8, width)
        own = lax.dynamic_index_in_dim(got, places[iteration], 0, keepdims=False, allow_negative_indices=False)
        green_row = jnp.sum(own, axis=0).reshape(points, 2, 2, 2, width)
        near_sum = jnp.sum(got, axis=(0, 1, 2))
        near_sum, green_row = lax.optimization_barrier((near_sum, green_row))
        sums = spread(jnp.broadcast_to(near_sum[None], (far, 8, width)), FAR, FAR_FIRST[iteration])
        sums, green_row = lax.optimization_barrier((sums, green_row))
        if iteration == ITERS - 1:
            return last_step(sums, green_row, column, point_count)
        local_green = (jnp.sum(sums, axis=0) / point_count).reshape(2, 2, 2, width)
        self_energy = jnp.stack(second_order(local_green, column), axis=0)


def solution(mesh):
    fine = Mesh(mesh.devices.reshape([n for _, n in CUT]), [name for name, _ in CUT])
    placed = (
        P(KA, None, None, None, TA, None),
        P(None, None, None, TA, None),
        P(KA, None, None, None, TA),
        P(KA, None, None, None),
        P(None, None, None, TA),
        P(None, None, None, TA),
    )
    return jax.shard_map(
        body,
        mesh=fine,
        in_specs=placed,
        out_specs=(P(KA, None, None, None, TA), P(None, None, None, TA)),
        check_vma=False,
    )
```

```python
import functools

import jax
import jax.numpy as jnp
from jax import lax
from jax.experimental import pallas as pl
from jax.experimental.pallas import tpu as pltpu
from jax.sharding import Mesh, PartitionSpec as P

ITERS = 2


TIME_STEP = 0.02
COUPLING = 1.0

CUT = (("y", 8), ("xh", 2), ("zh", 4), ("zl", 2), ("xl", 2), ("core", 2))
KA = ("y", "xh", "zh", "zl")
TA = ("xl", "core")
NEAR = ("zl", "xh")
FAR = ("y", "zh")
NEAR_FIRST = (13, 13)
FAR_FIRST = (18, 18)


def second_order(local_green, column):
    green_real = local_green[0]
    green_imag = local_green[1]
    square_real = green_real * green_real - green_imag * green_imag
    square_imag = 2.0 * green_real * green_imag
    real_part = square_real * column[0] - square_imag * column[1]
    imag_part = square_real * column[1] + square_imag * column[0]
    return COUPLING * COUPLING * real_part, COUPLING * COUPLING * imag_part


def spread(blocks, axes, first):
    order = [rank ^ first for rank in range(lax.axis_size(axes))]
    return lax.all_to_all(blocks, axes, 0, 0, tiled=True, axis_index_groups=[order])


def parts_of(ref, index, o, r, b):
    part = ref[(*index, pl.ds(b, 1), slice(None))]
    return -part if (o == 0 and r == 1) else part


def fill_left(sigma_ref, row_ref, sigma_lhs, row_lhs):
    points, width = row_ref.shape[0], row_ref.shape[-1]
    sigma_lhs[...] = jnp.zeros_like(sigma_lhs)
    row_lhs[...] = jnp.zeros_like(row_lhs)
    for o in range(2):
        for a in range(2):
            for j in range(4):
                r, b = j // 2, j % 2
                lanes = pl.ds(j * width, width)
                part = parts_of(sigma_ref, (o ^ r, a), o, r, b)
                for c in range(2):
                    sigma_lhs[c, pl.ds(c * 4 + o * 2 + a, 1), lanes] = part
                for k in range(points):
                    part = parts_of(row_ref, (k, o ^ r, a), o, r, b)
                    for c in range(2):
                        row_lhs[c, pl.ds(k * 8 + c * 4 + o * 2 + a, 1), lanes] = part


def contract(left, blocks):
    total = None
    for c in range(2):
        right = jnp.concatenate([blocks[j][c] for j in range(4)], axis=0)
        term = jnp.dot(left[c].astype(jnp.bfloat16), right, preferred_element_type=jnp.float32)
        total = term if total is None else total + term
    return total


def propagate_share(near, times, first, k, inner, prev, factors, out_ref):
    width = prev.shape[-1]
    place = lax.broadcasted_iota(jnp.int32, (8, width), 0)
    own_time = lax.axis_index(TA)
    for t in range(times):
        part = TIME_STEP * inner[:, t * width:(t + 1) * width]
        part = part + jnp.where(own_time == t, prev, 0.0)
        share = None
        for j in range(4):
            low = jnp.broadcast_to(part[j:j + 1], (8, width))
            high = jnp.broadcast_to(part[4 + j:5 + j], (8, width))
            term = factors[j] * jnp.where(place < 4, low, high)
            share = term if share is None else share + term
        for n in range(near):
            for c in range(2):
                out_ref[n * times + (t ^ first), pl.ds(k * 8 + c, 4, stride=2), :] = share[c * 4:(c + 1) * 4]


def first_kernel(
    near, times, first,
    prop_in, sigma_in, prev_in, green_in, hist_in,
    out_ref, factor_ref, own_prev, green_buf, hist_buf,
    prop_ref, sigma_ref, prev_ref, sigma_lhs, row_lhs, small, sems,
):
    points, width = prev_ref.shape[0], prev_ref.shape[-1]
    little = [
        pltpu.make_async_copy(src, dst, small.at[i])
        for i, (src, dst) in enumerate(((sigma_in, sigma_ref), (prev_in, prev_ref), (prop_in, prop_ref)))
    ]
    for copy in little:
        copy.start()
    large = {}
    for j in range(4):
        large[points, j] = pltpu.make_async_copy(hist_in.at[j // 2, j % 2], hist_buf.at[j], sems.at[points, j])
        large[points, j].start()
    for k in range(points):
        for j in range(4):
            large[k, j] = pltpu.make_async_copy(green_in.at[k, j // 2, j % 2], green_buf.at[k, j], sems.at[k, j])
            large[k, j].start(priority=1)
    for copy in little:
        copy.wait()
    fill_left(sigma_ref, prev_ref, sigma_lhs, row_lhs)
    for k in range(points):
        for o in range(2):
            for a in range(2):
                for c in range(2):
                    own_prev[pl.ds(k * 8 + c * 4 + o * 2 + a, 1), :] = prev_ref[k, o, a, pl.ds(c, 1), :]
    for k in range(points):
        for r in range(2):
            for a in range(2):
                for b in range(2):
                    entry = jnp.broadcast_to(prop_ref[k, r, pl.ds(a, 1), pl.ds(b, 1)], (1, width))
                    for o in range(2):
                        value = -entry if (o == 1 and r == 1) else entry
                        for c in range(2):
                            factor_ref[k, o * 2 + b, pl.ds(c * 4 + (o ^ r) * 2 + a, 1), :] = value
    for j in range(4):
        large[points, j].wait()
    row_terms = contract(row_lhs, [[hist_buf[j, c] for c in range(2)] for j in range(4)])
    for k in range(points):
        for j in range(4):
            large[k, j].wait()
        inner = contract(sigma_lhs, [[green_buf[k, j, c] for c in range(2)] for j in range(4)])
        inner = inner + row_terms[k * 8:(k + 1) * 8]
        factors = [factor_ref[k, j] for j in range(4)]
        propagate_share(near, times, first, k, inner, own_prev[pl.ds(k * 8, 8), :], factors, out_ref)


def next_kernel(
    near, times, first,
    sigma_ref, row_ref, factor_ref, own_prev, green_ref, hist_ref, out_ref,
    sigma_lhs, row_lhs,
):
    points = row_ref.shape[0]
    fill_left(sigma_ref, row_ref, sigma_lhs, row_lhs)
    row_terms = contract(row_lhs, [[hist_ref[j, c] for c in range(2)] for j in range(4)])
    for k in range(points):
        inner = contract(sigma_lhs, [[green_ref[k, j, c] for c in range(2)] for j in range(4)])
        inner = inner + row_terms[k * 8:(k + 1) * 8]
        factors = [factor_ref[k, j] for j in range(4)]
        propagate_share(near, times, first, k, inner, own_prev[pl.ds(k * 8, 8), :], factors, out_ref)


def last_kernel(
    point_count, sums_ref, row_ref, column_ref, row_out, energy_out, energy_ref, local_ref, sems,
):
    row_copy = pltpu.make_async_copy(row_ref, row_out, sems.at[0])
    row_copy.start()
    local_ref[...] = jnp.sum(sums_ref[...], axis=0) / point_count
    for a in range(2):
        local = [local_ref[pl.ds(o * 4 + a * 2, 2), :] for o in range(2)]
        parts = second_order(local, [column_ref[o, a] for o in range(2)])
        for o in range(2):
            energy_ref[o, a] = parts[o]
    energy_copy = pltpu.make_async_copy(energy_ref, energy_out, sems.at[1])
    energy_copy.start()
    row_copy.wait()
    energy_copy.wait()


VMEM = pl.BlockSpec(memory_space=pltpu.VMEM)
HBM = pl.BlockSpec(memory_space=pltpu.HBM)


def left_scratch(points, width):
    return [
        pltpu.VMEM((2, 8, 4 * width), jnp.float32),
        pltpu.VMEM((2, points * 8, 4 * width), jnp.float32),
    ]


def first_share(propagator, self_energy, prev_row, green_hist, sigma_hist, near, times, first):
    points, width = prev_row.shape[0], prev_row.shape[-1]
    full = sigma_hist.shape[-1]
    return pl.pallas_call(
        functools.partial(first_kernel, near, times, first),
        out_shape=(
            jax.ShapeDtypeStruct((near * times, points * 8, width), jnp.float32),
            jax.ShapeDtypeStruct((points, 4, 8, width), jnp.float32),
            jax.ShapeDtypeStruct((points * 8, width), jnp.float32),
            jax.ShapeDtypeStruct((points, 4, 2, width, full), jnp.bfloat16),
            jax.ShapeDtypeStruct((4, 2, width, full), jnp.bfloat16),
        ),
        in_specs=[HBM] * 5,
        out_specs=(VMEM,) * 5,
        scratch_shapes=[
            pltpu.VMEM(propagator.shape, jnp.float32),
            pltpu.VMEM(self_energy.shape, jnp.float32),
            pltpu.VMEM(prev_row.shape, jnp.float32),
            *left_scratch(points, width),
            pltpu.SemaphoreType.DMA((3,)),
            pltpu.SemaphoreType.DMA((points + 1, 4)),
        ],
        compiler_params=pltpu.CompilerParams(vmem_limit_bytes=16 << 20),
        name="first_share",
    )(*(
        pltpu.with_memory_space_constraint(x, pltpu.HBM)
        for x in (propagator, self_energy, prev_row, green_hist, sigma_hist)
    ))


def next_share(self_energy, green_row, factors, own_prev, green_hist, sigma_hist, near, times, first):
    points, width = green_row.shape[0], green_row.shape[-1]
    return pl.pallas_call(
        functools.partial(next_kernel, near, times, first),
        out_shape=jax.ShapeDtypeStruct((near * times, points * 8, width), jnp.float32),
        in_specs=[VMEM] * 6,
        out_specs=VMEM,
        scratch_shapes=left_scratch(points, width),
        compiler_params=pltpu.CompilerParams(vmem_limit_bytes=16 << 20),
        name="next_share",
    )(self_energy, green_row, factors, own_prev, green_hist, sigma_hist)


def last_step(sums, green_row, column, point_count):
    return pl.pallas_call(
        functools.partial(last_kernel, point_count),
        out_shape=(
            jax.ShapeDtypeStruct(green_row.shape, jnp.float32),
            jax.ShapeDtypeStruct(column.shape, jnp.float32),
        ),
        in_specs=[VMEM] * 3,
        out_specs=(HBM,) * 2,
        scratch_shapes=[
            pltpu.VMEM(column.shape, jnp.float32),
            pltpu.VMEM(sums.shape[1:], jnp.float32),
            pltpu.SemaphoreType.DMA((2,)),
        ],
        compiler_params=pltpu.CompilerParams(vmem_limit_bytes=16 << 20),
        name="last_step",
    )(sums, green_row, column)


def body(green_hist, sigma_hist, prev_row, propagator, impurity_column, sigma_start):
    points, width = prev_row.shape[0], prev_row.shape[-1]
    times = lax.axis_size(TA)
    near, far = lax.axis_size(NEAR), lax.axis_size(FAR)
    point_count = points * lax.axis_size(KA)
    places = [lax.axis_index(NEAR) ^ (first // times) for first in NEAR_FIRST]
    column = impurity_column
    for iteration in range(ITERS):
        first = NEAR_FIRST[iteration] % times
        if iteration == 0:
            share, factors, own_prev, green_held, hist_held = first_share(
                propagator, sigma_start, prev_row, green_hist, sigma_hist, near, times, first
            )
        else:
            share = next_share(
                self_energy, green_row, factors, own_prev, green_held, hist_held, near, times, first
            )
        share, *places = lax.optimization_barrier((share, *places))
        got = spread(share, NEAR + TA, NEAR_FIRST[iteration])
        got, column = lax.optimization_barrier((got, column))
        got = got.reshape(near, times, points, 8, width)
        own = lax.dynamic_index_in_dim(got, places[iteration], 0, keepdims=False, allow_negative_indices=False)
        green_row = jnp.sum(own, axis=0).reshape(points, 2, 2, 2, width)
        near_sum = jnp.sum(got, axis=(0, 1, 2))
        near_sum, green_row = lax.optimization_barrier((near_sum, green_row))
        sums = spread(jnp.broadcast_to(near_sum[None], (far, 8, width)), FAR, FAR_FIRST[iteration])
        sums, green_row = lax.optimization_barrier((sums, green_row))
        if iteration == ITERS - 1:
            return last_step(sums, green_row, column, point_count)
        local_green = (jnp.sum(sums, axis=0) / point_count).reshape(2, 2, 2, width)
        self_energy = jnp.stack(second_order(local_green, column), axis=0)


def solution(mesh):
    fine = Mesh(mesh.devices.reshape([n for _, n in CUT]), [name for name, _ in CUT])
    placed = (
        P(KA, None, None, None, TA, None),
        P(None, None, None, TA, None),
        P(KA, None, None, None, TA),
        P(KA, None, None, None),
        P(None, None, None, TA),
        P(None, None, None, TA),
    )
    return jax.shard_map(
        body,
        mesh=fine,
        in_specs=placed,
        out_specs=(P(KA, None, None, None, TA), P(None, None, None, TA)),
        check_vma=False,
    )
```

```python
import functools

import jax
import jax.numpy as jnp
from jax import lax
from jax.experimental import pallas as pl
from jax.experimental.pallas import tpu as pltpu
from jax.sharding import Mesh, PartitionSpec as P

ITERS = 2


TIME_STEP = 0.02
COUPLING = 1.0

CUT = (("y", 8), ("xh", 2), ("zh", 4), ("zl", 2), ("xl", 2), ("core", 2))
KA = ("y", "xh", "zh", "zl")
TA = ("xl", "core")
NEAR = ("zl", "xh")
FAR = ("y", "zh")
NEAR_FIRST = (13, 13)
FAR_FIRST = (18, 18)


def second_order(local_green, column):
    green_real = local_green[0]
    green_imag = local_green[1]
    square_real = green_real * green_real - green_imag * green_imag
    square_imag = 2.0 * green_real * green_imag
    real_part = square_real * column[0] - square_imag * column[1]
    imag_part = square_real * column[1] + square_imag * column[0]
    return COUPLING * COUPLING * real_part, COUPLING * COUPLING * imag_part


def spread(blocks, axes, first):
    order = [rank ^ first for rank in range(lax.axis_size(axes))]
    return lax.all_to_all(blocks, axes, 0, 0, tiled=True, axis_index_groups=[order])


def parts_of(ref, index, o, r, b):
    part = ref[(*index, pl.ds(b, 1), slice(None))]
    return -part if (o == 0 and r == 1) else part


def fill_left(sigma_ref, row_ref, sigma_lhs, row_lhs):
    points, width = row_ref.shape[0], row_ref.shape[-1]
    sigma_lhs[...] = jnp.zeros_like(sigma_lhs)
    row_lhs[...] = jnp.zeros_like(row_lhs)
    for o in range(2):
        for a in range(2):
            for j in range(4):
                r, b = j // 2, j % 2
                lanes = pl.ds(j * width, width)
                part = parts_of(sigma_ref, (o ^ r, a), o, r, b)
                for c in range(2):
                    sigma_lhs[c, pl.ds(c * 4 + o * 2 + a, 1), lanes] = part
                for k in range(points):
                    part = parts_of(row_ref, (k, o ^ r, a), o, r, b)
                    for c in range(2):
                        row_lhs[c, pl.ds(k * 8 + c * 4 + o * 2 + a, 1), lanes] = part


def contract(left, blocks):
    total = None
    for c in range(2):
        right = jnp.concatenate([blocks[j][c] for j in range(4)], axis=0)
        term = jnp.dot(left[c].astype(jnp.bfloat16), right, preferred_element_type=jnp.float32)
        total = term if total is None else total + term
    return total


def propagate_share(near, times, first, k, inner, prev, factors, out_ref):
    width = prev.shape[-1]
    place = lax.broadcasted_iota(jnp.int32, (8, width), 0)
    own_time = lax.axis_index(TA)
    for t in range(times):
        part = TIME_STEP * inner[:, t * width:(t + 1) * width]
        part = part + jnp.where(own_time == t, prev, 0.0)
        share = None
        for j in range(4):
            low = jnp.broadcast_to(part[j:j + 1], (8, width))
            high = jnp.broadcast_to(part[4 + j:5 + j], (8, width))
            term = factors[j] * jnp.where(place < 4, low, high)
            share = term if share is None else share + term
        for n in range(near):
            for c in range(2):
                out_ref[n * times + (t ^ first), pl.ds(k * 8 + c, 4, stride=2), :] = share[c * 4:(c + 1) * 4]


def first_kernel(
    near, times, first,
    prop_in, sigma_in, prev_in, green_in, hist_in,
    out_ref, factor_ref, own_prev, green_buf, hist_buf,
    prop_ref, sigma_ref, prev_ref, sigma_lhs, row_lhs, small, sems,
):
    points, width = prev_ref.shape[0], prev_ref.shape[-1]
    little = [
        pltpu.make_async_copy(src, dst, small.at[i])
        for i, (src, dst) in enumerate(((sigma_in, sigma_ref), (prev_in, prev_ref), (prop_in, prop_ref)))
    ]
    for copy in little:
        copy.start()
    large = {}
    for j in range(4):
        large[points, j] = pltpu.make_async_copy(hist_in.at[j // 2, j % 2], hist_buf.at[j], sems.at[points, j])
        large[points, j].start()
    for k in range(points):
        for j in range(4):
            large[k, j] = pltpu.make_async_copy(green_in.at[k, j // 2, j % 2], green_buf.at[k, j], sems.at[k, j])
            large[k, j].start(priority=1)
    for copy in little:
        copy.wait()
    fill_left(sigma_ref, prev_ref, sigma_lhs, row_lhs)
    for k in range(points):
        for o in range(2):
            for a in range(2):
                for c in range(2):
                    own_prev[pl.ds(k * 8 + c * 4 + o * 2 + a, 1), :] = prev_ref[k, o, a, pl.ds(c, 1), :]
    for k in range(points):
        for r in range(2):
            for a in range(2):
                for b in range(2):
                    entry = jnp.broadcast_to(prop_ref[k, r, pl.ds(a, 1), pl.ds(b, 1)], (1, width))
                    for o in range(2):
                        value = -entry if (o == 1 and r == 1) else entry
                        for c in range(2):
                            factor_ref[k, o * 2 + b, pl.ds(c * 4 + (o ^ r) * 2 + a, 1), :] = value
    for j in range(4):
        large[points, j].wait()
    row_terms = contract(row_lhs, [[hist_buf[j, c] for c in range(2)] for j in range(4)])
    for k in range(points):
        for j in range(4):
            large[k, j].wait()
        inner = contract(sigma_lhs, [[green_buf[k, j, c] for c in range(2)] for j in range(4)])
        inner = inner + row_terms[k * 8:(k + 1) * 8]
        factors = [factor_ref[k, j] for j in range(4)]
        propagate_share(near, times, first, k, inner, own_prev[pl.ds(k * 8, 8), :], factors, out_ref)


def fill_energy(point_count, sums_ref, column_ref, local_ref, energy_ref):
    local_ref[...] = jnp.sum(sums_ref[...], axis=0) / point_count
    for a in range(2):
        local = [local_ref[pl.ds(o * 4 + a * 2, 2), :] for o in range(2)]
        parts = second_order(local, [column_ref[o, a] for o in range(2)])
        for o in range(2):
            energy_ref[o, a] = parts[o]


def next_kernel(
    near, times, first, point_count,
    sums_ref, column_ref, row_ref, factor_ref, own_prev, green_ref, hist_ref, out_ref,
    sigma_lhs, row_lhs, local_ref, sigma_ref,
):
    points = row_ref.shape[0]
    fill_energy(point_count, sums_ref, column_ref, local_ref, sigma_ref)
    fill_left(sigma_ref, row_ref, sigma_lhs, row_lhs)
    row_terms = contract(row_lhs, [[hist_ref[j, c] for c in range(2)] for j in range(4)])
    for k in range(points):
        inner = contract(sigma_lhs, [[green_ref[k, j, c] for c in range(2)] for j in range(4)])
        inner = inner + row_terms[k * 8:(k + 1) * 8]
        factors = [factor_ref[k, j] for j in range(4)]
        propagate_share(near, times, first, k, inner, own_prev[pl.ds(k * 8, 8), :], factors, out_ref)


def last_kernel(
    point_count, sums_ref, row_ref, column_ref, row_out, energy_out, energy_ref, local_ref, sems,
):
    row_copy = pltpu.make_async_copy(row_ref, row_out, sems.at[0])
    row_copy.start()
    fill_energy(point_count, sums_ref, column_ref, local_ref, energy_ref)
    energy_copy = pltpu.make_async_copy(energy_ref, energy_out, sems.at[1])
    energy_copy.start()
    row_copy.wait()
    energy_copy.wait()


VMEM = pl.BlockSpec(memory_space=pltpu.VMEM)
HBM = pl.BlockSpec(memory_space=pltpu.HBM)


def left_scratch(points, width):
    return [
        pltpu.VMEM((2, 8, 4 * width), jnp.float32),
        pltpu.VMEM((2, points * 8, 4 * width), jnp.float32),
    ]


def first_share(propagator, self_energy, prev_row, green_hist, sigma_hist, near, times, first):
    points, width = prev_row.shape[0], prev_row.shape[-1]
    full = sigma_hist.shape[-1]
    return pl.pallas_call(
        functools.partial(first_kernel, near, times, first),
        out_shape=(
            jax.ShapeDtypeStruct((near * times, points * 8, width), jnp.float32),
            jax.ShapeDtypeStruct((points, 4, 8, width), jnp.float32),
            jax.ShapeDtypeStruct((points * 8, width), jnp.float32),
            jax.ShapeDtypeStruct((points, 4, 2, width, full), jnp.bfloat16),
            jax.ShapeDtypeStruct((4, 2, width, full), jnp.bfloat16),
        ),
        in_specs=[HBM] * 5,
        out_specs=(VMEM,) * 5,
        scratch_shapes=[
            pltpu.VMEM(propagator.shape, jnp.float32),
            pltpu.VMEM(self_energy.shape, jnp.float32),
            pltpu.VMEM(prev_row.shape, jnp.float32),
            *left_scratch(points, width),
            pltpu.SemaphoreType.DMA((3,)),
            pltpu.SemaphoreType.DMA((points + 1, 4)),
        ],
        compiler_params=pltpu.CompilerParams(vmem_limit_bytes=16 << 20),
        name="first_share",
    )(*(
        pltpu.with_memory_space_constraint(x, pltpu.HBM)
        for x in (propagator, self_energy, prev_row, green_hist, sigma_hist)
    ))


def next_share(sums, column, point_count, green_row, factors, own_prev, green_hist, sigma_hist, near, times, first):
    points, width = green_row.shape[0], green_row.shape[-1]
    return pl.pallas_call(
        functools.partial(next_kernel, near, times, first, point_count),
        out_shape=jax.ShapeDtypeStruct((near * times, points * 8, width), jnp.float32),
        in_specs=[VMEM] * 7,
        out_specs=VMEM,
        scratch_shapes=[
            *left_scratch(points, width),
            pltpu.VMEM(sums.shape[1:], jnp.float32),
            pltpu.VMEM(column.shape, jnp.float32),
        ],
        compiler_params=pltpu.CompilerParams(vmem_limit_bytes=16 << 20),
        name="next_share",
    )(sums, column, green_row, factors, own_prev, green_hist, sigma_hist)


def last_step(sums, green_row, column, point_count):
    return pl.pallas_call(
        functools.partial(last_kernel, point_count),
        out_shape=(
            jax.ShapeDtypeStruct(green_row.shape, jnp.float32),
            jax.ShapeDtypeStruct(column.shape, jnp.float32),
        ),
        in_specs=[VMEM] * 3,
        out_specs=(HBM,) * 2,
        scratch_shapes=[
            pltpu.VMEM(column.shape, jnp.float32),
            pltpu.VMEM(sums.shape[1:], jnp.float32),
            pltpu.SemaphoreType.DMA((2,)),
        ],
        compiler_params=pltpu.CompilerParams(vmem_limit_bytes=16 << 20),
        name="last_step",
    )(sums, green_row, column)


def body(green_hist, sigma_hist, prev_row, propagator, impurity_column, sigma_start):
    points, width = prev_row.shape[0], prev_row.shape[-1]
    times = lax.axis_size(TA)
    near, far = lax.axis_size(NEAR), lax.axis_size(FAR)
    point_count = points * lax.axis_size(KA)
    places = [lax.axis_index(NEAR) ^ (first // times) for first in NEAR_FIRST]
    column = impurity_column
    for iteration in range(ITERS):
        first = NEAR_FIRST[iteration] % times
        if iteration == 0:
            share, factors, own_prev, green_held, hist_held = first_share(
                propagator, sigma_start, prev_row, green_hist, sigma_hist, near, times, first
            )
        else:
            share = next_share(
                sums, column, point_count, green_row, factors, own_prev, green_held, hist_held, near, times, first
            )
        share, *places = lax.optimization_barrier((share, *places))
        got = spread(share, NEAR + TA, NEAR_FIRST[iteration])
        got, column = lax.optimization_barrier((got, column))
        got = got.reshape(near, times, points, 8, width)
        own = lax.dynamic_index_in_dim(got, places[iteration], 0, keepdims=False, allow_negative_indices=False)
        green_row = jnp.sum(own, axis=0).reshape(points, 2, 2, 2, width)
        near_sum = jnp.sum(got, axis=(0, 1, 2))
        near_sum, green_row = lax.optimization_barrier((near_sum, green_row))
        sums = spread(jnp.broadcast_to(near_sum[None], (far, 8, width)), FAR, FAR_FIRST[iteration])
        sums, green_row = lax.optimization_barrier((sums, green_row))
    return last_step(sums, green_row, column, point_count)


def solution(mesh):
    fine = Mesh(mesh.devices.reshape([n for _, n in CUT]), [name for name, _ in CUT])
    placed = (
        P(KA, None, None, None, TA, None),
        P(None, None, None, TA, None),
        P(KA, None, None, None, TA),
        P(KA, None, None, None),
        P(None, None, None, TA),
        P(None, None, None, TA),
    )
    return jax.shard_map(
        body,
        mesh=fine,
        in_specs=placed,
        out_specs=(P(KA, None, None, None, TA), P(None, None, None, TA)),
        check_vma=False,
    )
```

```python
import functools

import jax
import jax.numpy as jnp
from jax import lax
from jax.experimental import pallas as pl
from jax.experimental.pallas import tpu as pltpu
from jax.sharding import Mesh, PartitionSpec as P

ITERS = 2


TIME_STEP = 0.02
COUPLING = 1.0

CUT = (("y", 8), ("xh", 2), ("zh", 4), ("zl", 2), ("xl", 2), ("core", 2))
KA = ("y", "xh", "zh", "zl")
TA = ("xl", "core")
NEAR = ("zl", "xh")
FAR = ("y", "zh")
NEAR_FIRST = (13, 13)
FAR_FIRST = (18, 18)


def second_order(local_green, column):
    green_real = local_green[0]
    green_imag = local_green[1]
    square_real = green_real * green_real - green_imag * green_imag
    square_imag = 2.0 * green_real * green_imag
    real_part = square_real * column[0] - square_imag * column[1]
    imag_part = square_real * column[1] + square_imag * column[0]
    return COUPLING * COUPLING * real_part, COUPLING * COUPLING * imag_part


def spread(blocks, axes, first):
    order = [rank ^ first for rank in range(lax.axis_size(axes))]
    return lax.all_to_all(blocks, axes, 0, 0, tiled=True, axis_index_groups=[order])


def parts_of(ref, index, o, r, b):
    part = ref[(*index, pl.ds(b, 1), slice(None))]
    return -part if (o == 0 and r == 1) else part


def fill_left(sigma_ref, row_ref, sigma_lhs, row_lhs):
    points, width = row_ref.shape[0], row_ref.shape[-1]
    sigma_lhs[...] = jnp.zeros_like(sigma_lhs)
    row_lhs[...] = jnp.zeros_like(row_lhs)
    for o in range(2):
        for a in range(2):
            for j in range(4):
                r, b = j // 2, j % 2
                lanes = pl.ds(j * width, width)
                part = parts_of(sigma_ref, (o ^ r, a), o, r, b)
                for c in range(2):
                    sigma_lhs[c, pl.ds(c * 4 + o * 2 + a, 1), lanes] = part
                for k in range(points):
                    part = parts_of(row_ref, (k, o ^ r, a), o, r, b)
                    for c in range(2):
                        row_lhs[c, pl.ds(k * 8 + c * 4 + o * 2 + a, 1), lanes] = part


def contract(left, blocks):
    total = None
    for c in range(2):
        right = jnp.concatenate([blocks[j][c] for j in range(4)], axis=0)
        term = jnp.dot(left[c].astype(jnp.bfloat16), right, preferred_element_type=jnp.float32)
        total = term if total is None else total + term
    return total


def propagate_share(near, times, first, k, inner, prev, factors, out_ref):
    width = prev.shape[-1]
    place = lax.broadcasted_iota(jnp.int32, (8, width), 0)
    own_time = lax.axis_index(TA)
    for t in range(times):
        part = TIME_STEP * inner[:, t * width:(t + 1) * width]
        part = part + jnp.where(own_time == t, prev, 0.0)
        share = None
        for j in range(4):
            low = jnp.broadcast_to(part[j:j + 1], (8, width))
            high = jnp.broadcast_to(part[4 + j:5 + j], (8, width))
            term = factors[j] * jnp.where(place < 4, low, high)
            share = term if share is None else share + term
        for n in range(near):
            for c in range(2):
                out_ref[n * times + (t ^ first), pl.ds(k * 8 + c, 4, stride=2), :] = share[c * 4:(c + 1) * 4]


def first_kernel(
    near, times, first,
    prop_in, sigma_in, prev_in, green_in, hist_in,
    out_ref, factor_ref, own_prev, green_buf, hist_buf,
    prop_ref, sigma_ref, prev_ref, sigma_lhs, row_lhs, small, sems,
):
    points, width = prev_ref.shape[0], prev_ref.shape[-1]
    little = [
        pltpu.make_async_copy(src, dst, small.at[i])
        for i, (src, dst) in enumerate(((sigma_in, sigma_ref), (prev_in, prev_ref), (prop_in, prop_ref)))
    ]
    for copy in little:
        copy.start()
    large = {}
    for j in range(4):
        large[points, j] = pltpu.make_async_copy(hist_in.at[j // 2, j % 2], hist_buf.at[j], sems.at[points, j])
        large[points, j].start()
    for k in range(points):
        for j in range(4):
            large[k, j] = pltpu.make_async_copy(green_in.at[k, j // 2, j % 2], green_buf.at[k, j], sems.at[k, j])
            large[k, j].start(priority=1)
    for copy in little:
        copy.wait()
    fill_left(sigma_ref, prev_ref, sigma_lhs, row_lhs)
    for k in range(points):
        for o in range(2):
            for a in range(2):
                for c in range(2):
                    own_prev[pl.ds(k * 8 + c * 4 + o * 2 + a, 1), :] = prev_ref[k, o, a, pl.ds(c, 1), :]
    for k in range(points):
        for r in range(2):
            for a in range(2):
                for b in range(2):
                    entry = jnp.broadcast_to(prop_ref[k, r, pl.ds(a, 1), pl.ds(b, 1)], (1, width))
                    for o in range(2):
                        value = -entry if (o == 1 and r == 1) else entry
                        for c in range(2):
                            factor_ref[k, o * 2 + b, pl.ds(c * 4 + (o ^ r) * 2 + a, 1), :] = value
    for j in range(4):
        large[points, j].wait()
    row_terms = contract(row_lhs, [[hist_buf[j, c] for c in range(2)] for j in range(4)])
    for k in range(points):
        for j in range(4):
            large[k, j].wait()
        inner = contract(sigma_lhs, [[green_buf[k, j, c] for c in range(2)] for j in range(4)])
        inner = inner + row_terms[k * 8:(k + 1) * 8]
        factors = [factor_ref[k, j] for j in range(4)]
        propagate_share(near, times, first, k, inner, own_prev[pl.ds(k * 8, 8), :], factors, out_ref)


def fill_energy(point_count, sums_ref, column_ref, local_ref, energy_ref):
    local_ref[...] = jnp.sum(sums_ref[...], axis=0) / point_count
    for a in range(2):
        local = [local_ref[pl.ds(o * 4 + a * 2, 2), :] for o in range(2)]
        parts = second_order(local, [column_ref[o, a] for o in range(2)])
        for o in range(2):
            energy_ref[o, a] = parts[o]


def next_kernel(
    near, times, first, point_count,
    sums_ref, column_ref, row_ref, factor_ref, own_prev, green_ref, hist_ref, out_ref,
    sigma_lhs, row_lhs, local_ref, sigma_ref,
):
    points = row_ref.shape[0]
    fill_energy(point_count, sums_ref, column_ref, local_ref, sigma_ref)
    fill_left(sigma_ref, row_ref, sigma_lhs, row_lhs)
    row_terms = contract(row_lhs, [[hist_ref[j, c] for c in range(2)] for j in range(4)])
    for k in range(points):
        inner = contract(sigma_lhs, [[green_ref[k, j, c] for c in range(2)] for j in range(4)])
        inner = inner + row_terms[k * 8:(k + 1) * 8]
        factors = [factor_ref[k, j] for j in range(4)]
        propagate_share(near, times, first, k, inner, own_prev[pl.ds(k * 8, 8), :], factors, out_ref)


def last_kernel(
    point_count, sums_ref, row_ref, column_ref, row_out, energy_out, energy_ref, local_ref, sems,
):
    row_copy = pltpu.make_async_copy(row_ref, row_out, sems.at[0])
    row_copy.start()
    fill_energy(point_count, sums_ref, column_ref, local_ref, energy_ref)
    energy_copy = pltpu.make_async_copy(energy_ref, energy_out, sems.at[1])
    energy_copy.start()
    row_copy.wait()
    energy_copy.wait()


VMEM = pl.BlockSpec(memory_space=pltpu.VMEM)
HBM = pl.BlockSpec(memory_space=pltpu.HBM)


def left_scratch(points, width):
    return [
        pltpu.VMEM((2, 8, 4 * width), jnp.float32),
        pltpu.VMEM((2, points * 8, 4 * width), jnp.float32),
    ]


def first_share(propagator, self_energy, prev_row, green_hist, sigma_hist, near, times, first):
    points, width = prev_row.shape[0], prev_row.shape[-1]
    full = sigma_hist.shape[-1]
    return pl.pallas_call(
        functools.partial(first_kernel, near, times, first),
        out_shape=(
            jax.ShapeDtypeStruct((near * times, points * 8, width), jnp.float32),
            jax.ShapeDtypeStruct((points, 4, 8, width), jnp.float32),
            jax.ShapeDtypeStruct((points * 8, width), jnp.float32),
            jax.ShapeDtypeStruct((points, 4, 2, width, full), jnp.bfloat16),
            jax.ShapeDtypeStruct((4, 2, width, full), jnp.bfloat16),
        ),
        in_specs=[HBM] * 5,
        out_specs=(VMEM,) * 5,
        scratch_shapes=[
            pltpu.VMEM(propagator.shape, jnp.float32),
            pltpu.VMEM(self_energy.shape, jnp.float32),
            pltpu.VMEM(prev_row.shape, jnp.float32),
            *left_scratch(points, width),
            pltpu.SemaphoreType.DMA((3,)),
            pltpu.SemaphoreType.DMA((points + 1, 4)),
        ],
        compiler_params=pltpu.CompilerParams(vmem_limit_bytes=16 << 20),
        name="first_share",
    )(*(
        pltpu.with_memory_space_constraint(x, pltpu.HBM)
        for x in (propagator, self_energy, prev_row, green_hist, sigma_hist)
    ))


def next_share(sums, column, point_count, green_row, factors, own_prev, green_hist, sigma_hist, near, times, first):
    points, width = green_row.shape[0], green_row.shape[-1]
    return pl.pallas_call(
        functools.partial(next_kernel, near, times, first, point_count),
        out_shape=jax.ShapeDtypeStruct((near * times, points * 8, width), jnp.float32),
        in_specs=[VMEM] * 7,
        out_specs=VMEM,
        scratch_shapes=[
            *left_scratch(points, width),
            pltpu.VMEM(sums.shape[1:], jnp.float32),
            pltpu.VMEM(column.shape, jnp.float32),
        ],
        compiler_params=pltpu.CompilerParams(vmem_limit_bytes=16 << 20),
        name="next_share",
    )(sums, column, green_row, factors, own_prev, green_hist, sigma_hist)


def last_step(sums, green_row, column, point_count):
    return pl.pallas_call(
        functools.partial(last_kernel, point_count),
        out_shape=(
            jax.ShapeDtypeStruct(green_row.shape, jnp.float32),
            jax.ShapeDtypeStruct(column.shape, jnp.float32),
        ),
        in_specs=[VMEM] * 3,
        out_specs=(HBM,) * 2,
        scratch_shapes=[
            pltpu.VMEM(column.shape, jnp.float32),
            pltpu.VMEM(sums.shape[1:], jnp.float32),
            pltpu.SemaphoreType.DMA((2,)),
        ],
        compiler_params=pltpu.CompilerParams(vmem_limit_bytes=16 << 20),
        name="last_step",
    )(sums, green_row, column)


def near_kernel(times, first, got_ref, sum_ref, row_ref):
    points = row_ref.shape[0]
    slot = lax.axis_index(NEAR) ^ (first // times)
    total = jnp.sum(got_ref[...], axis=0)
    total = sum(total[k * 8:(k + 1) * 8] for k in range(points))
    sum_ref[...] = jnp.broadcast_to(total[None], sum_ref.shape)
    own = jnp.sum(got_ref[pl.ds(slot * times, times)], axis=0)
    for k in range(points):
        for o in range(2):
            for a in range(2):
                at = k * 8 + o * 4 + a * 2
                row_ref[k, o, a] = own[at:at + 2]


def near_step(got, points, times, far, first):
    width = got.shape[-1]
    return pl.pallas_call(
        functools.partial(near_kernel, times, first),
        out_shape=(
            jax.ShapeDtypeStruct((far, 8, width), jnp.float32),
            jax.ShapeDtypeStruct((points, 2, 2, 2, width), jnp.float32),
        ),
        in_specs=[VMEM],
        out_specs=(VMEM,) * 2,
        compiler_params=pltpu.CompilerParams(vmem_limit_bytes=16 << 20),
        name="near_step",
    )(got)


def body(green_hist, sigma_hist, prev_row, propagator, impurity_column, sigma_start):
    points, width = prev_row.shape[0], prev_row.shape[-1]
    times = lax.axis_size(TA)
    near, far = lax.axis_size(NEAR), lax.axis_size(FAR)
    point_count = points * lax.axis_size(KA)
    column = impurity_column
    for iteration in range(ITERS):
        first = NEAR_FIRST[iteration] % times
        if iteration == 0:
            share, factors, own_prev, green_held, hist_held = first_share(
                propagator, sigma_start, prev_row, green_hist, sigma_hist, near, times, first
            )
        else:
            share = next_share(
                sums, column, point_count, green_row, factors, own_prev, green_held, hist_held, near, times, first
            )
        got = spread(share, NEAR + TA, NEAR_FIRST[iteration])
        got, column = lax.optimization_barrier((got, column))
        near_sum, green_row = near_step(got, points, times, far, NEAR_FIRST[iteration])
        near_sum, green_row = lax.optimization_barrier((near_sum, green_row))
        sums = spread(near_sum, FAR, FAR_FIRST[iteration])
        sums, green_row = lax.optimization_barrier((sums, green_row))
    return last_step(sums, green_row, column, point_count)


def solution(mesh):
    fine = Mesh(mesh.devices.reshape([n for _, n in CUT]), [name for name, _ in CUT])
    placed = (
        P(KA, None, None, None, TA, None),
        P(None, None, None, TA, None),
        P(KA, None, None, None, TA),
        P(KA, None, None, None),
        P(None, None, None, TA),
        P(None, None, None, TA),
    )
    return jax.shard_map(
        body,
        mesh=fine,
        in_specs=placed,
        out_specs=(P(KA, None, None, None, TA), P(None, None, None, TA)),
        check_vma=False,
    )
```

```python
import functools

import jax
import jax.numpy as jnp
from jax import lax
from jax.experimental import pallas as pl
from jax.experimental.pallas import tpu as pltpu
from jax.sharding import Mesh, PartitionSpec as P

ITERS = 2


TIME_STEP = 0.02
COUPLING = 1.0

CUT = (("y", 8), ("xh", 2), ("zh", 4), ("zl", 2), ("xl", 2), ("core", 2))
KA = ("y", "xh", "zh", "zl")
TA = ("xl", "core")
NEAR = ("zl", "xh")
FAR = ("y", "zh")
NEAR_FIRST = (13, 13)
FAR_FIRST = (19, 18)


def second_order(local_green, column):
    green_real = local_green[0]
    green_imag = local_green[1]
    square_real = green_real * green_real - green_imag * green_imag
    square_imag = 2.0 * green_real * green_imag
    real_part = square_real * column[0] - square_imag * column[1]
    imag_part = square_real * column[1] + square_imag * column[0]
    return COUPLING * COUPLING * real_part, COUPLING * COUPLING * imag_part


def spread(blocks, axes, first):
    order = [rank ^ first for rank in range(lax.axis_size(axes))]
    return lax.all_to_all(blocks, axes, 0, 0, tiled=True, axis_index_groups=[order])


def parts_of(ref, index, o, r, b):
    part = ref[(*index, pl.ds(b, 1), slice(None))]
    return -part if (o == 0 and r == 1) else part


def fill_left(sigma_ref, row_ref, sigma_lhs, row_lhs):
    points, width = row_ref.shape[0], row_ref.shape[-1]
    sigma_lhs[...] = jnp.zeros_like(sigma_lhs)
    row_lhs[...] = jnp.zeros_like(row_lhs)
    for o in range(2):
        for a in range(2):
            for j in range(4):
                r, b = j // 2, j % 2
                lanes = pl.ds(j * width, width)
                part = parts_of(sigma_ref, (o ^ r, a), o, r, b)
                for c in range(2):
                    sigma_lhs[c, pl.ds(c * 4 + o * 2 + a, 1), lanes] = part
                for k in range(points):
                    part = parts_of(row_ref, (k, o ^ r, a), o, r, b)
                    for c in range(2):
                        row_lhs[c, pl.ds(k * 8 + c * 4 + o * 2 + a, 1), lanes] = part


def contract(left, blocks):
    total = None
    for c in range(2):
        right = jnp.concatenate([blocks[j][c] for j in range(4)], axis=0)
        term = jnp.dot(left[c].astype(jnp.bfloat16), right, preferred_element_type=jnp.float32)
        total = term if total is None else total + term
    return total


def propagate_share(near, times, first, k, inner, prev, factors, out_ref):
    width = prev.shape[-1]
    place = lax.broadcasted_iota(jnp.int32, (8, width), 0)
    own_time = lax.axis_index(TA)
    for t in range(times):
        part = TIME_STEP * inner[:, t * width:(t + 1) * width]
        part = part + jnp.where(own_time == t, prev, 0.0)
        share = None
        for j in range(4):
            low = jnp.broadcast_to(part[j:j + 1], (8, width))
            high = jnp.broadcast_to(part[4 + j:5 + j], (8, width))
            term = factors[j] * jnp.where(place < 4, low, high)
            share = term if share is None else share + term
        for n in range(near):
            for c in range(2):
                out_ref[n * times + (t ^ first), pl.ds(k * 8 + c, 4, stride=2), :] = share[c * 4:(c + 1) * 4]


def first_kernel(
    near, times, first,
    prop_in, sigma_in, prev_in, green_in, hist_in,
    out_ref, factor_ref, own_prev, green_buf, hist_buf,
    prop_ref, sigma_ref, prev_ref, sigma_lhs, row_lhs, small, sems,
):
    points, width = prev_ref.shape[0], prev_ref.shape[-1]
    little = [
        pltpu.make_async_copy(src, dst, small.at[i])
        for i, (src, dst) in enumerate(((sigma_in, sigma_ref), (prev_in, prev_ref), (prop_in, prop_ref)))
    ]
    for copy in little:
        copy.start()
    large = {}
    for j in range(4):
        large[points, j] = pltpu.make_async_copy(hist_in.at[j // 2, j % 2], hist_buf.at[j], sems.at[points, j])
        large[points, j].start()
    for k in range(points):
        for j in range(4):
            large[k, j] = pltpu.make_async_copy(green_in.at[k, j // 2, j % 2], green_buf.at[k, j], sems.at[k, j])
            large[k, j].start(priority=1)
    for copy in little:
        copy.wait()
    fill_left(sigma_ref, prev_ref, sigma_lhs, row_lhs)
    for k in range(points):
        for o in range(2):
            for a in range(2):
                for c in range(2):
                    own_prev[pl.ds(k * 8 + c * 4 + o * 2 + a, 1), :] = prev_ref[k, o, a, pl.ds(c, 1), :]
    for k in range(points):
        for r in range(2):
            for a in range(2):
                for b in range(2):
                    entry = jnp.broadcast_to(prop_ref[k, r, pl.ds(a, 1), pl.ds(b, 1)], (1, width))
                    for o in range(2):
                        value = -entry if (o == 1 and r == 1) else entry
                        for c in range(2):
                            factor_ref[k, o * 2 + b, pl.ds(c * 4 + (o ^ r) * 2 + a, 1), :] = value
    for j in range(4):
        large[points, j].wait()
    row_terms = contract(row_lhs, [[hist_buf[j, c] for c in range(2)] for j in range(4)])
    for k in range(points):
        for j in range(4):
            large[k, j].wait()
        inner = contract(sigma_lhs, [[green_buf[k, j, c] for c in range(2)] for j in range(4)])
        inner = inner + row_terms[k * 8:(k + 1) * 8]
        factors = [factor_ref[k, j] for j in range(4)]
        propagate_share(near, times, first, k, inner, own_prev[pl.ds(k * 8, 8), :], factors, out_ref)


def fill_energy(point_count, sums_ref, column_ref, local_ref, energy_ref):
    local_ref[...] = jnp.sum(sums_ref[...], axis=0) / point_count
    for a in range(2):
        local = [local_ref[pl.ds(o * 4 + a * 2, 2), :] for o in range(2)]
        parts = second_order(local, [column_ref[o, a] for o in range(2)])
        for o in range(2):
            energy_ref[o, a] = parts[o]


def next_kernel(
    near, times, first, point_count,
    sums_ref, column_ref, row_ref, factor_ref, own_prev, green_ref, hist_ref, out_ref,
    sigma_lhs, row_lhs, local_ref, sigma_ref,
):
    points = row_ref.shape[0]
    fill_energy(point_count, sums_ref, column_ref, local_ref, sigma_ref)
    fill_left(sigma_ref, row_ref, sigma_lhs, row_lhs)
    row_terms = contract(row_lhs, [[hist_ref[j, c] for c in range(2)] for j in range(4)])
    for k in range(points):
        inner = contract(sigma_lhs, [[green_ref[k, j, c] for c in range(2)] for j in range(4)])
        inner = inner + row_terms[k * 8:(k + 1) * 8]
        factors = [factor_ref[k, j] for j in range(4)]
        propagate_share(near, times, first, k, inner, own_prev[pl.ds(k * 8, 8), :], factors, out_ref)


def last_kernel(
    point_count, sums_ref, row_ref, column_ref, row_out, energy_out, energy_ref, local_ref, sems,
):
    row_copy = pltpu.make_async_copy(row_ref, row_out, sems.at[0])
    row_copy.start()
    fill_energy(point_count, sums_ref, column_ref, local_ref, energy_ref)
    energy_copy = pltpu.make_async_copy(energy_ref, energy_out, sems.at[1])
    energy_copy.start()
    row_copy.wait()
    energy_copy.wait()


VMEM = pl.BlockSpec(memory_space=pltpu.VMEM)
HBM = pl.BlockSpec(memory_space=pltpu.HBM)


def left_scratch(points, width):
    return [
        pltpu.VMEM((2, 8, 4 * width), jnp.float32),
        pltpu.VMEM((2, points * 8, 4 * width), jnp.float32),
    ]


def first_share(propagator, self_energy, prev_row, green_hist, sigma_hist, near, times, first):
    points, width = prev_row.shape[0], prev_row.shape[-1]
    full = sigma_hist.shape[-1]
    return pl.pallas_call(
        functools.partial(first_kernel, near, times, first),
        out_shape=(
            jax.ShapeDtypeStruct((near * times, points * 8, width), jnp.float32),
            jax.ShapeDtypeStruct((points, 4, 8, width), jnp.float32),
            jax.ShapeDtypeStruct((points * 8, width), jnp.float32),
            jax.ShapeDtypeStruct((points, 4, 2, width, full), jnp.bfloat16),
            jax.ShapeDtypeStruct((4, 2, width, full), jnp.bfloat16),
        ),
        in_specs=[HBM] * 5,
        out_specs=(VMEM,) * 5,
        scratch_shapes=[
            pltpu.VMEM(propagator.shape, jnp.float32),
            pltpu.VMEM(self_energy.shape, jnp.float32),
            pltpu.VMEM(prev_row.shape, jnp.float32),
            *left_scratch(points, width),
            pltpu.SemaphoreType.DMA((3,)),
            pltpu.SemaphoreType.DMA((points + 1, 4)),
        ],
        compiler_params=pltpu.CompilerParams(vmem_limit_bytes=16 << 20),
        name="first_share",
    )(*(
        pltpu.with_memory_space_constraint(x, pltpu.HBM)
        for x in (propagator, self_energy, prev_row, green_hist, sigma_hist)
    ))


def next_share(sums, column, point_count, green_row, factors, own_prev, green_hist, sigma_hist, near, times, first):
    points, width = green_row.shape[0], green_row.shape[-1]
    return pl.pallas_call(
        functools.partial(next_kernel, near, times, first, point_count),
        out_shape=jax.ShapeDtypeStruct((near * times, points * 8, width), jnp.float32),
        in_specs=[VMEM] * 7,
        out_specs=VMEM,
        scratch_shapes=[
            *left_scratch(points, width),
            pltpu.VMEM(sums.shape[1:], jnp.float32),
            pltpu.VMEM(column.shape, jnp.float32),
        ],
        compiler_params=pltpu.CompilerParams(vmem_limit_bytes=16 << 20),
        name="next_share",
    )(sums, column, green_row, factors, own_prev, green_hist, sigma_hist)


def last_step(sums, green_row, column, point_count):
    return pl.pallas_call(
        functools.partial(last_kernel, point_count),
        out_shape=(
            jax.ShapeDtypeStruct(green_row.shape, jnp.float32),
            jax.ShapeDtypeStruct(column.shape, jnp.float32),
        ),
        in_specs=[VMEM] * 3,
        out_specs=(HBM,) * 2,
        scratch_shapes=[
            pltpu.VMEM(column.shape, jnp.float32),
            pltpu.VMEM(sums.shape[1:], jnp.float32),
            pltpu.SemaphoreType.DMA((2,)),
        ],
        compiler_params=pltpu.CompilerParams(vmem_limit_bytes=16 << 20),
        name="last_step",
    )(sums, green_row, column)


def body(green_hist, sigma_hist, prev_row, propagator, impurity_column, sigma_start):
    points, width = prev_row.shape[0], prev_row.shape[-1]
    times = lax.axis_size(TA)
    near, far = lax.axis_size(NEAR), lax.axis_size(FAR)
    point_count = points * lax.axis_size(KA)
    places = [lax.axis_index(NEAR) ^ (first // times) for first in NEAR_FIRST]
    column = impurity_column
    for iteration in range(ITERS):
        first = NEAR_FIRST[iteration] % times
        if iteration == 0:
            share, factors, own_prev, green_held, hist_held = first_share(
                propagator, sigma_start, prev_row, green_hist, sigma_hist, near, times, first
            )
        else:
            share = next_share(
                sums, column, point_count, green_row, factors, own_prev, green_held, hist_held, near, times, first
            )
        share, *places = lax.optimization_barrier((share, *places))
        got = spread(share, NEAR + TA, NEAR_FIRST[iteration])
        got, column = lax.optimization_barrier((got, column))
        got = got.reshape(near, times, points, 8, width)
        own = lax.dynamic_index_in_dim(got, places[iteration], 0, keepdims=False, allow_negative_indices=False)
        green_row = jnp.sum(own, axis=0).reshape(points, 2, 2, 2, width)
        near_sum = jnp.sum(got, axis=(0, 1, 2))
        near_sum, green_row = lax.optimization_barrier((near_sum, green_row))
        sums = spread(jnp.broadcast_to(near_sum[None], (far, 8, width)), FAR, FAR_FIRST[iteration])
        sums, green_row = lax.optimization_barrier((sums, green_row))
    return last_step(sums, green_row, column, point_count)


def solution(mesh):
    fine = Mesh(mesh.devices.reshape([n for _, n in CUT]), [name for name, _ in CUT])
    placed = (
        P(KA, None, None, None, TA, None),
        P(None, None, None, TA, None),
        P(KA, None, None, None, TA),
        P(KA, None, None, None),
        P(None, None, None, TA),
        P(None, None, None, TA),
    )
    return jax.shard_map(
        body,
        mesh=fine,
        in_specs=placed,
        out_specs=(P(KA, None, None, None, TA), P(None, None, None, TA)),
        check_vma=False,
    )
```
